256 devices in a mesh: gx: 16 (over x, y), gy: 16 (over z, core).
Axes of the slice: x: 4, y: 4, z: 8, core: 2. Of those that a mesh axis runs over, the one named last changes fastest.
Arguments:
- permeability: float32 [1, 16, 128, 2048], P(None, None, 'gx', 'gy'), may hold values from 0.2 to 5
- saturation: float32 [1, 16, 128, 2048], P(None, None, 'gx', 'gy'), may hold values from 0.1 to 0.9
- pressure_old: float32 [1, 16, 128, 2048], P(None, None, 'gx', 'gy'), may hold values from -6 to 6
- source: float32 [16, 128, 2048], P(None, 'gx', 'gy'), may hold values from -25 to 25
Outputs:
- pressure: float32 [1, 16, 128, 2048], P(None, None, 'gx', 'gy')
- saturation_new: float32 [1, 16, 128, 2048], P(None, None, 'gx', 'gy')
The draws below stay inside these ranges and needn't reach their ends.
All inputs are finite; a program needn't handle non-finite values.
Results may differ from the reference program's by a relative error of at most 0.0003.
Values sent between devices are 32-bit elements; how exact they have to be, the bound alone decides.
No kernel may reach another device: no remote copies, remote signals or barrier semaphores. Data moves between devices by JAX's collectives and lax.ppermute only.
A program may use at most 64 MiB of HBM per device.

```python
import math
import jax
import jax.numpy as jnp
from jax import lax

SAMPLES = 1
NZ = 16
ITERS = 2
NX = 128
NY = 2048


def draw_source(key, part):
    across = jnp.arange(NX, dtype=jnp.float32) / max(NX - 1, 1)
    along = jnp.arange(NY, dtype=jnp.float32) / max(NY - 1, 1)
    growth = 3.0
    noise_field = jnp.clip(jax.random.normal(key, (NZ, NX, NY), jnp.float32), -5.0, 5.0)
    slope_factor = jnp.power(growth, across)[:, None] * jnp.power(growth, along)[None, :]
    return 0.5 * slope_factor[None] * noise_field


def levels(key, shape, shards, least, largest):
    def one(axis_at, shards_of):
        heights = jax.random.uniform(jax.random.fold_in(jax.random.fold_in(key, 6), axis_at), (shards_of,), jnp.float32, least / len(shards), largest / len(shards))
        return jnp.repeat(jnp.exp(heights), shape[axis_at] // shards_of).reshape((-1,) + (1,) * (len(shape) - axis_at - 1))

    loudness = one(*shards[0])
    for cut in shards[1:]:
        loudness = loudness * one(*cut)
    return loudness


def scatter_about(key, extent, deviation, reach, shards=(), kind=jnp.bfloat16):
    result = deviation * jax.random.normal(key, extent, jnp.float32)
    if shards:
        result = result * levels(key, extent, shards, -0.22, 0.18)
    return jnp.clip(result, -reach, reach).astype(kind)


def setup_inputs(seed: int = 0) -> dict:
    arg_keys = jax.random.split(jax.random.key(seed), 5)
    permeability = jnp.clip(jnp.exp(math.log(5.0) - 3.218876 * jax.random.uniform(arg_keys[0], (SAMPLES, NZ, NX, NY), jnp.float32) ** levels(arg_keys[0], (SAMPLES, NZ, NX, NY), ((2, 16), (3, 16)), -0.2, 0.2)), 0.2, 5.0)
    saturation = jnp.clip(0.1 + 0.79999997 * jax.random.uniform(arg_keys[1], (SAMPLES, NZ, NX, NY), jnp.float32) ** levels(arg_keys[1], (SAMPLES, NZ, NX, NY), ((2, 16), (3, 16)), -0.2, 0.2), 0.1, 0.9)
    pressure_old = scatter_about(arg_keys[2], (SAMPLES, NZ, NX, NY), 1.0, 6.0, ((2, 16), (3, 16)), jnp.float32)
    source = draw_source(jax.random.fold_in(arg_keys[4], 71), 0)
    return dict(permeability=permeability, saturation=saturation, pressure_old=pressure_old, source=source)


storage_term = 0.5
vertical_ratio = 0.1
step_ratio = 0.05
water_viscosity = 1.0
oil_viscosity = 2.0


def total_mobility(values):
    return values * values / water_viscosity + (1.0 - values) * (1.0 - values) / oil_viscosity


def water_fraction(values):
    return (values * values / water_viscosity) / total_mobility(values)


def neighbours(values, layout_axis):
    widths = [(0, 0)] * values.ndim
    widths[layout_axis] = (1, 1)
    padded = jnp.pad(values, widths)
    length = padded.shape[layout_axis]
    return lax.slice_in_dim(padded, 0, length - 1, axis=layout_axis), lax.slice_in_dim(padded, 1, length, axis=layout_axis)


def upper_part(values, layout_axis):
    length = values.shape[layout_axis]
    return lax.slice_in_dim(values, 1, length, axis=layout_axis)


def lower_part(values, layout_axis):
    length = values.shape[layout_axis]
    return lax.slice_in_dim(values, 0, length - 1, axis=layout_axis)


def coefficient(perm_left, perm_right, mobile_left, mobile_right, scaling):
    return scaling * (2.0 * perm_left * perm_right / (perm_left + perm_right)) * (0.5 * (mobile_left + mobile_right))


def face_terms(permeability, saturation):
    terms = []
    for layout_axis in (1, 2, 3):
        perm_left, perm_right = neighbours(permeability, layout_axis)
        sat_left, sat_right = neighbours(saturation, layout_axis)
        scaling = vertical_ratio if layout_axis == 1 else 1.0
        terms.append(coefficient(perm_left, perm_right, total_mobility(sat_left), total_mobility(sat_right), scaling))
    return terms


def divergence(flows):
    summed = None
    for layout_axis, flow in zip((1, 2, 3), flows):
        change = upper_part(flow, layout_axis) - lower_part(flow, layout_axis)
        summed = change if summed is None else summed + change
    return summed


def diagonal_of(terms):
    summed = storage_term
    for layout_axis, term in zip((1, 2, 3), terms):
        summed = summed + (upper_part(term, layout_axis) + lower_part(term, layout_axis))
    return summed


def fluxes(terms, values):
    flows = []
    for layout_axis, term in zip((1, 2, 3), terms):
        left_side, right_side = neighbours(values, layout_axis)
        flows.append(term * (left_side - right_side))
    return flows


def apply_operator(terms, values):
    return storage_term * values + divergence(fluxes(terms, values))


def sample_dot(former, latter):
    return jnp.sum(former * latter, axis=(1, 2, 3), keepdims=True)


def transport(flows, current, inflow_rate):
    fraction = water_fraction(current)
    water = []
    for layout_axis, flow in zip((1, 2, 3), flows):
        frac_left, frac_right = neighbours(fraction, layout_axis)
        water.append(flow * jnp.where(flow > 0.0, frac_left, frac_right))
    gained = jnp.maximum(inflow_rate, 0.0) + jnp.minimum(inflow_rate, 0.0) * fraction
    return current + step_ratio * (gained - divergence(water))


def reference(permeability, saturation, pressure_old, source):
    terms = face_terms(permeability, saturation)
    diagonal = diagonal_of(terms)
    inflow_rate = source[None]
    right_side = inflow_rate + storage_term * pressure_old
    solution = pressure_old
    residual = right_side - apply_operator(terms, solution)
    precond = residual / diagonal
    direction = precond
    energy_now = sample_dot(residual, precond)
    for sweep in range(ITERS):
        image_field = apply_operator(terms, direction)
        step_size = energy_now / sample_dot(direction, image_field)
        solution = solution + step_size * direction
        residual = residual - step_size * image_field
        precond = residual / diagonal
        energy_next = sample_dot(residual, precond)
        direction = precond + (energy_next / energy_now) * direction
        energy_now = energy_next
    flows = fluxes(terms, solution)
    current = saturation
    for sweep in range(2):
        current = transport(flows, current, inflow_rate)
    return solution, current
```

```python
import jax
import jax.numpy as jnp
from jax import lax
from jax.sharding import PartitionSpec as P

storage_term = 0.5
vertical_ratio = 0.1
step_ratio = 0.05
water_viscosity = 1.0
oil_viscosity = 2.0

HALO = 4


def padded(x, axis, dim, width):
    size, length = lax.axis_size(axis), x.shape[dim]
    up = [(i, i + 1) for i in range(size - 1)]
    down = [(i + 1, i) for i in range(size - 1)]
    last = lax.slice_in_dim(x, length - width, length, axis=dim)
    first = lax.slice_in_dim(x, 0, width, axis=dim)
    before = lax.ppermute(last, axis, up)
    after = lax.ppermute(first, axis, down)
    return jnp.concatenate([before, x, after], axis=dim)


def total_mobility(s):
    return s * s / water_viscosity + (1.0 - s) * (1.0 - s) / oil_viscosity


def pairs(x, dim):
    n = x.shape[dim]
    return lax.slice_in_dim(x, 0, n - 1, axis=dim), lax.slice_in_dim(x, 1, n, axis=dim)


def coefficient(perm, mobile, dim, scaling):
    ka, kb = pairs(perm, dim)
    ma, mb = pairs(mobile, dim)
    summed = ka + kb
    safe = jnp.where(summed > 0.0, summed, 1.0)
    return scaling * (2.0 * ka * kb / safe) * (0.5 * (ma + mb))


def both_sides(face, dim):
    widths = [(0, 0)] * face.ndim
    widths[dim] = (1, 1)
    return pairs(jnp.pad(face, widths), dim)


def divergence(faces):
    total = None
    for dim, face in enumerate(faces):
        lower, upper = both_sides(face, dim)
        change = upper - lower
        total = change if total is None else total + change
    return total


def fluxes(terms, v):
    out = []
    for dim, term in enumerate(terms):
        a, b = pairs(v, dim)
        out.append(term * (a - b))
    return out


def apply_operator(terms, v):
    return storage_term * v + divergence(fluxes(terms, v))


def transport(flows, s, rate):
    fraction = s * s / water_viscosity / total_mobility(s)
    water = []
    for dim, flow in enumerate(flows):
        a, b = pairs(fraction, dim)
        water.append(flow * jnp.where(flow > 0.0, a, b))
    gained = jnp.maximum(rate, 0.0) + jnp.minimum(rate, 0.0) * fraction
    return s + step_ratio * (gained - divergence(water))


def one_sample(permeability, saturation, pressure_old, source):
    stacked = jnp.stack([permeability, saturation, pressure_old, source])
    wide = padded(padded(stacked, "gx", 2, HALO), "gy", 3, HALO)
    perm, sat, old, rate = wide[0], wide[1], wide[2], wide[3]
    mobile = total_mobility(sat)
    terms = [coefficient(perm, mobile, dim, vertical_ratio if dim == 0 else 1.0) for dim in range(3)]
    diagonal = storage_term
    for dim, term in enumerate(terms):
        lower, upper = both_sides(term, dim)
        diagonal = diagonal + (upper + lower)
    residual = rate + storage_term * old - apply_operator(terms, old)
    first = residual / diagonal
    image = apply_operator(terms, first)
    second = (image - residual) / diagonal
    second_image = apply_operator(terms, second)
    own = lambda x: x[:, HALO:-HALO, HALO:-HALO]
    r, z, g, v, w = (own(x) for x in (residual, first, image, second, second_image))
    partial = jnp.stack([jnp.sum(t) for t in (r * z, z * g, z * (g - r), v * g, v * w)])
    size = lax.axis_size("gx") * lax.axis_size("gy")
    row = jnp.pad(partial, (0, 123))
    sums = lax.all_to_all(jnp.broadcast_to(row, (size, 128)), ("gx", "gy"), 0, 0, tiled=True).sum(0)
    rz, zaz, rv, vaz, vav = (sums[i] for i in range(5))
    ratio = vaz / zaz
    bottom = vav - ratio * vaz
    top = rv - ratio * rz
    b = jnp.where(bottom > 0.0, top / bottom, 0.0)
    a = rz / zaz - b * ratio
    new = old + a * first + b * second
    flows = fluxes(terms, new)
    s = transport(flows, sat, rate)
    s = transport(flows, s, rate)
    return own(new), own(s)


def local(permeability, saturation, pressure_old, source):
    outs = [one_sample(permeability[i], saturation[i], pressure_old[i], source) for i in range(permeability.shape[0])]
    return jnp.stack([o[0] for o in outs]), jnp.stack([o[1] for o in outs])


def solution(mesh):
    field = P(None, None, "gx", "gy")
    return jax.shard_map(local, mesh=mesh, in_specs=(field, field, field, P(None, "gx", "gy")), out_specs=(field, field), check_vma=False)
```

```python
import jax
import jax.numpy as jnp
from jax import lax
from jax.experimental import pallas as pl
from jax.experimental.pallas import tpu as pltpu
from jax.sharding import PartitionSpec as P

storage_term = 0.5
vertical_ratio = 0.1
step_ratio = 0.05
water_viscosity = 1.0
oil_viscosity = 2.0

NZ, ROWS, LANES, HALO = 16, 8, 128, 4
SPAN = 2 * ROWS
SEG = 16
TILES = NZ * SEG // LANES
PER = LANES // SEG
F32 = jnp.float32


def lanes(shape=(ROWS, LANES)):
    return lax.broadcasted_iota(jnp.int32, shape, len(shape) - 1)


def sublanes(shape=(ROWS, LANES)):
    return lax.broadcasted_iota(jnp.int32, shape, len(shape) - 2)


def turn(x, by, axis):
    n = x.shape[axis]
    if isinstance(by, int):
        by %= n
        if by == 0:
            return x
    return pltpu.roll(x, by, axis)


def total_mobility(s):
    return s * s / water_viscosity + (1.0 - s) * (1.0 - s) / oil_viscosity


def water_fraction(s):
    return s * s / water_viscosity / total_mobility(s)


def coefficient(ka, kb, ma, mb):
    return ka * kb * (ma + mb) / jnp.maximum(ka + kb, 1e-30)


def row_next(x):
    return turn(x, -1, 0)


def row_prev(x):
    return turn(x, 1, 0)


def col_next(x):
    return turn(x, -1, 1)


def col_prev(x):
    return turn(x, 1, 1)


def pack_columns(k, s, p, q, to_prev, to_next):
    seg = lanes() % SEG // 4
    layer = lanes() // SEG
    for t in range(TILES):
        first = jnp.zeros((ROWS, LANES), F32)
        last = jnp.zeros((ROWS, LANES), F32)
        for zz in range(PER):
            for i, ref in enumerate((k, s, p, q)):
                x = ref[t * PER + zz]
                here = (layer == zz) & (seg == i)
                at = zz * SEG + 4 * i
                first = jnp.where(here, turn(x, at, 1), first)
                last = jnp.where(here, turn(x, at + HALO, 1), last)
        to_prev[t] = first
        to_next[t] = last


def pack_rows(k, s, p, q, own_first, own_last, from_prev, from_next, packed, to_prev, to_next):
    seg = lanes() % SEG // 4
    low = sublanes() < HALO

    def pair(at, a, b):
        to_prev[at] = jnp.where(low, a, turn(b, HALO, 0))
        to_next[at] = jnp.where(low, turn(a, HALO, 0), b)

    for t in range(TILES):
        cols = []
        for i in range(4):
            x = turn(from_prev[t], -4 * i, 1)
            x = jnp.where(seg == 1, turn(own_first[t], 4 - 4 * i, 1), x)
            x = jnp.where(seg == 2, turn(own_last[t], 8 - 4 * i, 1), x)
            x = jnp.where(seg == 3, turn(from_next[t], 12 - 4 * i, 1), x)
            packed[i, t] = x
            cols.append(x)
        pair(2 * NZ + t, cols[0], cols[1])
        pair(2 * NZ + TILES + t, cols[2], cols[3])

    for z in range(NZ):
        pair(z, k[z], s[z])
        pair(NZ + z, p[z], q[z])


def layer_next(x):
    edge = lanes((SPAN, LANES)) < LANES - SEG
    moved = [turn(t, -SEG, 1) for t in x]
    return [jnp.where(edge, moved[i], moved[(i + 1) % TILES]) for i in range(TILES)]


def layer_prev(x):
    edge = lanes((SPAN, LANES)) >= SEG
    moved = [turn(t, SEG, 1) for t in x]
    return [jnp.where(edge, moved[i], moved[(i - 1) % TILES]) for i in range(TILES)]


def each(f, *args):
    return [f(*a) for a in zip(*args)]


def packed_divergence(flows):
    fx, fy, fz = flows
    return each(lambda x, xp, y, yp, z, zp: (z - zp) + (x - xp) + (y - yp), fx, each(row_prev, fx), fy, each(col_prev, fy), fz, layer_prev(fz))


def packed_flows(terms, v):
    nexts = (each(row_next, v), each(col_next, v), layer_next(v))
    return [each(lambda c, a, b: c * (a - b), term, v, n) for term, n in zip(terms, nexts)]


def edge_next(y, packed_face, z):
    at = LANES - 1 - (z % PER * SEG + 11)
    return jnp.where(lanes((SPAN, LANES)) == LANES - 1, pltpu.roll(packed_face[z // PER], at, 1), y)


def edge_prev(y, packed_face, z):
    at = LANES - (z % PER * SEG + 3)
    return jnp.where(lanes((SPAN, LANES)) == 0, pltpu.roll(packed_face[z // PER], at, 1), col_prev(y))


def middle(k_own, s_own, p_own, q_own, packed, prev, nxt,
           sums, z0, v, s, q, fp, fz, fv, s_pack, q_pack, fp_pack, fz_pack, fv_pack,
           k, p, cx, cy, cz, inv, r, cy_pack):
    gx, gy = lax.axis_index("gx"), lax.axis_index("gy")
    last_gx, last_gy = lax.axis_size("gx") - 1, lax.axis_size("gy") - 1
    row8 = sublanes()
    low = row8 < HALO
    inside_rows = jnp.where(low, jnp.where(gx == last_gx, 0.0, 1.0), jnp.where(gx == 0, 0.0, 1.0))
    seg8 = lanes() % SEG // 4
    inside_cols = jnp.where(seg8 == 0, jnp.where(gy == 0, 0.0, 1.0), jnp.where(seg8 == 3, jnp.where(gy == last_gy, 0.0, 1.0), 1.0))

    def halo_rows(at):
        below, above = nxt[at], prev[at]
        return jnp.where(low, below, turn(above, HALO, 0)), jnp.where(low, turn(below, HALO, 0), above)

    def assemble(z, _):
        ka, sa = halo_rows(z)
        pa, qa = halo_rows(NZ + z)
        k[z, :ROWS], k[z, ROWS:] = k_own[z], ka * inside_rows
        s[z, :ROWS], s[z, ROWS:] = s_own[z], sa
        p[z, :ROWS], p[z, ROWS:] = p_own[z], pa
        q[z, :ROWS], q[z, ROWS:] = q_own[z], qa
        return _

    lax.fori_loop(0, NZ, assemble, 0)

    kp, sp, pp, qp = [], [], [], []
    for t in range(TILES):
        ka, sa = halo_rows(2 * NZ + t)
        pa, qa = halo_rows(2 * NZ + TILES + t)
        kp.append(jnp.concatenate([packed[0, t] * inside_cols, ka * inside_rows * inside_cols], 0))
        sp.append(jnp.concatenate([packed[1, t], sa], 0))
        pp.append(jnp.concatenate([packed[2, t], pa], 0))
        qp.append(jnp.concatenate([packed[3, t], qa], 0))
    mp = each(total_mobility, sp)
    tx = each(coefficient, kp, each(row_next, kp), mp, each(row_next, mp))
    ty = each(coefficient, kp, each(col_next, kp), mp, each(col_next, mp))
    tz = each(coefficient, kp, layer_next(kp), mp, layer_next(mp))
    tz = each(lambda c: vertical_ratio * c, tz)
    tz[-1] = jnp.where(lanes((SPAN, LANES)) < LANES - SEG, tz[-1], 0.0)
    terms = (tx, ty, tz)
    diag = each(lambda x, xp, y, yp, z, zp: storage_term + (z + zp) + (x + xp) + (y + yp), tx, each(row_prev, tx), ty, each(col_prev, ty), tz, layer_prev(tz))
    ip = each(lambda d: 1.0 / d, diag)
    flows_p = packed_flows(terms, pp)
    rp = each(lambda a, d: a - d, qp, packed_divergence(flows_p))
    zp0 = each(lambda a, b: a * b, rp, ip)
    flows_z = packed_flows(terms, zp0)
    gp = each(lambda a, d: storage_term * a + d, zp0, packed_divergence(flows_z))
    vp = each(lambda a, b, c: (a - b) * c, gp, rp, ip)
    flows_v = packed_flows(terms, vp)
    for t in range(TILES):
        s_pack[t], q_pack[t], cy_pack[t] = sp[t], qp[t], ty[t]
        for d in range(3):
            fp_pack[d, t], fz_pack[d, t], fv_pack[d, t] = flows_p[d][t], flows_z[d][t], flows_v[d][t]

    def first(z, carry):
        cz_prev, fz_prev = carry
        up = jnp.minimum(z + 1, NZ - 1)
        kz, pz, m = k[z], p[z], total_mobility(s[z])
        mx = row_next(m)
        ax = coefficient(kz, row_next(kz), m, mx)
        ay = edge_next(coefficient(kz, col_next(kz), m, col_next(m)), cy_pack, z)
        az = jnp.where(z < NZ - 1, vertical_ratio, 0.0) * coefficient(kz, k[up], m, total_mobility(s[up]))
        d = storage_term + (az + cz_prev) + (ax + row_prev(ax)) + (ay + edge_prev(ay, cy_pack, z))
        fx = ax * (pz - row_next(pz))
        fy = edge_next(ay * (pz - col_next(pz)), fp_pack.at[1], z)
        fzz = az * (pz - p[up])
        res = q[z] - ((fzz - fz_prev) + (fx - row_prev(fx)) + (fy - edge_prev(fy, fp_pack.at[1], z)))
        inverse = 1.0 / d
        cx[z], cy[z], cz[z], inv[z], r[z] = ax, ay, az, inverse, res
        fp[0, z], fp[1, z], fp[2, z] = fx, fy, fzz
        z0[z] = res * inverse
        return az, fzz

    zero = jnp.zeros((SPAN, LANES), F32)
    zero8 = jnp.zeros((ROWS, LANES), F32)
    lax.fori_loop(0, NZ, first, (zero, zero))

    def second(z, carry):
        fz_prev, rz, zaz, rv, vaz = carry
        up = jnp.minimum(z + 1, NZ - 1)
        a = z0[z]
        fx = cx[z] * (a - row_next(a))
        fy = edge_next(cy[z] * (a - col_next(a)), fz_pack.at[1], z)
        fzz = cz[z] * (a - z0[up])
        g = storage_term * a + ((fzz - fz_prev) + (fx - row_prev(fx)) + (fy - edge_prev(fy, fz_pack.at[1], z)))
        fz[0, z], fz[1, z], fz[2, z] = fx, fy, fzz
        diff = g - r[z]
        b = diff * inv[z]
        v[z] = b
        a8, g8, d8, b8, r8 = a[:ROWS], g[:ROWS], diff[:ROWS], b[:ROWS], r[z, :ROWS]
        return fzz, rz + r8 * a8, zaz + a8 * g8, rv + a8 * d8, vaz + b8 * g8

    _, rz, zaz, rv, vaz = lax.fori_loop(0, NZ, second, (zero, zero8, zero8, zero8, zero8))

    def third(z, carry):
        fz_prev, vav = carry
        up = jnp.minimum(z + 1, NZ - 1)
        a = v[z]
        fx = cx[z] * (a - row_next(a))
        fy = edge_next(cy[z] * (a - col_next(a)), fv_pack.at[1], z)
        fzz = cz[z] * (a - v[up])
        fv[0, z], fv[1, z], fv[2, z] = fx, fy, fzz
        w = storage_term * a + ((fzz - fz_prev) + (fx - row_prev(fx)) + (fy - edge_prev(fy, fv_pack.at[1], z)))
        return fzz, vav + a[:ROWS] * w[:ROWS]

    _, vav = lax.fori_loop(0, NZ, third, (zero, zero8))
    row = zero8
    for i, x in enumerate((rz, zaz, rv, vaz, vav)):
        row = jnp.where(lanes() == i, jnp.sum(x), row)
    for i in range(sums.shape[0] // ROWS):
        sums[i * ROWS:(i + 1) * ROWS] = row


def finish(sums, p_own, z0, v, s, q, fp, fz, fv, s_pack, q_pack, fp_pack, fz_pack, fv_pack,
           pressure, s_new, flow, f1, s1, wy0_pack, wy1_pack, f0):
    total = jnp.sum(sums[...], axis=0, keepdims=True)
    lane = lanes((1, LANES))
    rz, zaz, rv, vaz, vav = (jnp.sum(jnp.where(lane == i, total, 0.0), axis=1, keepdims=True) for i in range(5))
    ratio = vaz / zaz
    bottom = vav - ratio * vaz
    top = rv - ratio * rz
    good = bottom > 0.0
    b = jnp.where(good, top / jnp.where(good, bottom, 1.0), 0.0)
    a = rz / zaz - b * ratio
    a16, b16 = (jnp.broadcast_to(x, (SPAN, LANES)) for x in (a, b))

    def gained(rate, fraction):
        return jnp.maximum(rate, 0.0) + jnp.minimum(rate, 0.0) * fraction

    def upwind(flux, here, there):
        return flux * jnp.where(flux > 0.0, here, there)

    flows = [[fp_pack[d, t] + a16 * fz_pack[d, t] + b16 * fv_pack[d, t] for t in range(TILES)] for d in range(3)]
    s_now = [s_pack[t] for t in range(TILES)]
    q_now = [q_pack[t] for t in range(TILES)]
    for step, keep in enumerate((wy0_pack, wy1_pack)):
        fr = each(water_fraction, s_now)
        nexts = (each(row_next, fr), each(col_next, fr), layer_next(fr))
        water = [each(upwind, fl, fr, n) for fl, n in zip(flows, nexts)]
        for t in range(TILES):
            keep[t] = water[1][t]
        if step == 0:
            s_now = each(lambda x, rate, f, d: x + step_ratio * (gained(rate, f) - d), s_now, q_now, fr, packed_divergence(water))

    def fractions(z, c):
        f0[z] = water_fraction(s[z])
        return c

    lax.fori_loop(0, NZ, fractions, 0)

    def first(z, wz_prev):
        up = jnp.minimum(z + 1, NZ - 1)
        fx, fy, fzz = (fp[d, z] + a16 * fz[d, z] + b16 * fv[d, z] for d in range(3))
        flow[0, z], flow[1, z], flow[2, z] = fx, fy, fzz
        pressure[z] = p_own[z] + a16[:ROWS] * z0[z, :ROWS] + b16[:ROWS] * v[z, :ROWS]
        f = f0[z]
        wx = upwind(fx, f, row_next(f))
        wy = edge_next(upwind(fy, f, col_next(f)), wy0_pack, z)
        wz = upwind(fzz, f, f0[up])
        new = s[z] + step_ratio * (gained(q[z], f) - ((wz - wz_prev) + (wx - row_prev(wx)) + (wy - edge_prev(wy, wy0_pack, z))))
        s1[z] = new
        f1[z] = water_fraction(new)
        return wz

    lax.fori_loop(0, NZ, first, jnp.zeros((SPAN, LANES), F32))

    def second(z, wz_prev):
        up = jnp.minimum(z + 1, NZ - 1)
        f = f1[z]
        wx = upwind(flow[0, z], f, row_next(f))
        wy = edge_next(upwind(flow[1, z], f, col_next(f)), wy1_pack, z)
        wz = upwind(flow[2, z, :ROWS], f[:ROWS], f1[up, :ROWS])
        east = (wy - edge_prev(wy, wy1_pack, z))[:ROWS]
        s_new[z] = s1[z, :ROWS] + step_ratio * (gained(q[z, :ROWS], f[:ROWS]) - ((wz - wz_prev) + (wx - row_prev(wx))[:ROWS] + east))
        return wz

    lax.fori_loop(0, NZ, second, jnp.zeros((ROWS, LANES), F32))


def call(body, out_shapes, args, scratch=()):
    vmem = pl.BlockSpec(memory_space=pltpu.VMEM)
    return pl.pallas_call(
        body,
        name=body.__name__,
        out_shape=tuple(jax.ShapeDtypeStruct(s, F32) for s in out_shapes),
        in_specs=[vmem] * len(args),
        out_specs=tuple(vmem for _ in out_shapes),
        scratch_shapes=[pltpu.VMEM(s, F32) for s in scratch],
    )(*args)


def ring(x, axis, by):
    n = lax.axis_size(axis)
    return lax.ppermute(x, axis, [(i, (i + by) % n) for i in range(n)])


def one_sample(k, s, p, q):
    assert k.shape == (NZ, ROWS, LANES)
    cols = (TILES, ROWS, LANES)
    first, last = call(pack_columns, (cols, cols), (k, s, p, q))
    from_prev, from_next = ring(last, "gy", 1), ring(first, "gy", -1)
    message = (2 * NZ + 2 * TILES, ROWS, LANES)
    packed, to_prev, to_next = call(pack_rows, ((4,) + cols, message, message), (k, s, p, q, first, last, from_prev, from_next))
    prev, nxt = ring(to_next, "gx", 1), ring(to_prev, "gx", -1)
    size = lax.axis_size("gx") * lax.axis_size("gy")
    field, strip = (NZ, SPAN, LANES), (TILES, SPAN, LANES)
    mid = call(
        middle,
        ((size, LANES),) + (field,) * 4 + ((3,) + field,) * 3 + (strip,) * 2 + ((3,) + strip,) * 3,
        (k, s, p, q, packed, prev, nxt),
        (field,) * 7 + (strip,),
    )
    sums = lax.all_to_all(mid[0], ("gx", "gy"), 0, 0, tiled=True)
    return call(finish, ((NZ, ROWS, LANES),) * 2, (sums, p) + tuple(mid[1:]), ((3,) + field, field, field, strip, strip, field))


def local(permeability, saturation, pressure_old, source):
    outs = [one_sample(permeability[i], saturation[i], pressure_old[i], source) for i in range(permeability.shape[0])]
    return jnp.stack([o[0] for o in outs]), jnp.stack([o[1] for o in outs])


def solution(mesh):
    field = P(None, None, "gx", "gy")
    return jax.shard_map(local, mesh=mesh, in_specs=(field, field, field, P(None, "gx", "gy")), out_specs=(field, field), check_vma=False)
```

```python
import jax
import jax.numpy as jnp
from jax import lax
from jax.experimental import pallas as pl
from jax.experimental.pallas import tpu as pltpu
from jax.sharding import PartitionSpec as P

storage_term = 0.5
vertical_ratio = 0.1
step_ratio = 0.05
water_viscosity = 1.0
oil_viscosity = 2.0

NZ, ROWS, LANES, HALO = 16, 8, 128, 4
SPAN = 2 * ROWS
SEG = 16
TILES = NZ * SEG // LANES
PER = LANES // SEG
F32 = jnp.float32


def lanes(shape=(ROWS, LANES)):
    return lax.broadcasted_iota(jnp.int32, shape, len(shape) - 1)


def sublanes(shape=(ROWS, LANES)):
    return lax.broadcasted_iota(jnp.int32, shape, len(shape) - 2)


def turn(x, by, axis):
    n = x.shape[axis]
    if isinstance(by, int):
        by %= n
        if by == 0:
            return x
    return pltpu.roll(x, by, axis)


def total_mobility(s):
    return s * s / water_viscosity + (1.0 - s) * (1.0 - s) / oil_viscosity


def water_fraction(s):
    return s * s / water_viscosity / total_mobility(s)


def coefficient(ka, kb, ma, mb):
    return ka * kb * (ma + mb) / jnp.maximum(ka + kb, 1e-30)


def row_next(x):
    return turn(x, -1, 0)


def row_prev(x):
    return turn(x, 1, 0)


def col_next(x):
    return turn(x, -1, 1)


def col_prev(x):
    return turn(x, 1, 1)


def pack_columns(k_in, s_in, p_in, q_in, to_prev, to_next, k, s, p, q, sems):
    copies = [pltpu.make_async_copy(a, b, sems.at[i]) for i, (a, b) in enumerate(((k_in, k), (s_in, s), (p_in, p), (q_in, q)))]
    for c in copies:
        c.start()
    seg = lanes() % SEG // 4
    layer = lanes() // SEG
    first = [jnp.zeros((ROWS, LANES), F32) for _ in range(TILES)]
    last = [jnp.zeros((ROWS, LANES), F32) for _ in range(TILES)]
    for i, ref in enumerate((k, s, p, q)):
        copies[i].wait()
        for t in range(TILES):
            for zz in range(PER):
                x = ref[t * PER + zz]
                here = (layer == zz) & (seg == i)
                at = zz * SEG + 4 * i
                first[t] = jnp.where(here, turn(x, at, 1), first[t])
                last[t] = jnp.where(here, turn(x, at + HALO, 1), last[t])
    for t in range(TILES):
        to_prev[t] = first[t]
        to_next[t] = last[t]


def pack_rows(k, s, p, q, own_first, own_last, from_prev, from_next, packed, to_prev, to_next):
    seg = lanes() % SEG // 4
    low = sublanes() < HALO

    def pair(at, a, b):
        to_prev[at] = jnp.where(low, a, turn(b, HALO, 0))
        to_next[at] = jnp.where(low, turn(a, HALO, 0), b)

    for t in range(TILES):
        cols = []
        for i in range(4):
            x = turn(from_prev[t], -4 * i, 1)
            x = jnp.where(seg == 1, turn(own_first[t], 4 - 4 * i, 1), x)
            x = jnp.where(seg == 2, turn(own_last[t], 8 - 4 * i, 1), x)
            x = jnp.where(seg == 3, turn(from_next[t], 12 - 4 * i, 1), x)
            packed[i, t] = x
            cols.append(x)
        pair(2 * NZ + t, cols[0], cols[1])
        pair(2 * NZ + TILES + t, cols[2], cols[3])

    for z in range(NZ):
        pair(z, k[z], s[z])
        pair(NZ + z, p[z], q[z])


def layer_next(x):
    edge = lanes((SPAN, LANES)) < LANES - SEG
    moved = [turn(t, -SEG, 1) for t in x]
    return [jnp.where(edge, moved[i], moved[(i + 1) % TILES]) for i in range(TILES)]


def layer_prev(x):
    edge = lanes((SPAN, LANES)) >= SEG
    moved = [turn(t, SEG, 1) for t in x]
    return [jnp.where(edge, moved[i], moved[(i - 1) % TILES]) for i in range(TILES)]


def each(f, *args):
    return [f(*a) for a in zip(*args)]


def packed_divergence(flows):
    fx, fy, fz = flows
    return each(lambda x, xp, y, yp, z, zp: (z - zp) + (x - xp) + (y - yp), fx, each(row_prev, fx), fy, each(col_prev, fy), fz, layer_prev(fz))


def packed_flows(terms, v):
    nexts = (each(row_next, v), each(col_next, v), layer_next(v))
    return [each(lambda c, a, b: c * (a - b), term, v, n) for term, n in zip(terms, nexts)]


def edge_next(y, packed_face, z):
    at = LANES - 1 - (z % PER * SEG + 11)
    return jnp.where(lanes((SPAN, LANES)) == LANES - 1, pltpu.roll(packed_face[z // PER], at, 1), y)


def edge_prev(y, packed_face, z):
    at = LANES - (z % PER * SEG + 3)
    return jnp.where(lanes((SPAN, LANES)) == 0, pltpu.roll(packed_face[z // PER], at, 1), col_prev(y))


def middle(k_own, s_own, p_own, q_own, packed, prev, nxt,
           sums, z0, v, s, q, fp, fz, fv, s_pack, q_pack, fp_pack, fz_pack, fv_pack,
           k, p, cx, cy, cz, inv, r, cy_pack):
    gx, gy = lax.axis_index("gx"), lax.axis_index("gy")
    last_gx, last_gy = lax.axis_size("gx") - 1, lax.axis_size("gy") - 1
    row8 = sublanes()
    low = row8 < HALO
    inside_rows = jnp.where(low, jnp.where(gx == last_gx, 0.0, 1.0), jnp.where(gx == 0, 0.0, 1.0))
    seg8 = lanes() % SEG // 4
    inside_cols = jnp.where(seg8 == 0, jnp.where(gy == 0, 0.0, 1.0), jnp.where(seg8 == 3, jnp.where(gy == last_gy, 0.0, 1.0), 1.0))

    def halo_rows(at):
        below, above = nxt[at], prev[at]
        return jnp.where(low, below, turn(above, HALO, 0)), jnp.where(low, turn(below, HALO, 0), above)

    def assemble(z, _):
        ka, sa = halo_rows(z)
        pa, qa = halo_rows(NZ + z)
        k[z, :ROWS], k[z, ROWS:] = k_own[z], ka * inside_rows
        s[z, :ROWS], s[z, ROWS:] = s_own[z], sa
        p[z, :ROWS], p[z, ROWS:] = p_own[z], pa
        q[z, :ROWS], q[z, ROWS:] = q_own[z], qa
        return _

    lax.fori_loop(0, NZ, assemble, 0, unroll=NZ // 2)

    kp, sp, pp, qp = [], [], [], []
    for t in range(TILES):
        ka, sa = halo_rows(2 * NZ + t)
        pa, qa = halo_rows(2 * NZ + TILES + t)
        kp.append(jnp.concatenate([packed[0, t] * inside_cols, ka * inside_rows * inside_cols], 0))
        sp.append(jnp.concatenate([packed[1, t], sa], 0))
        pp.append(jnp.concatenate([packed[2, t], pa], 0))
        qp.append(jnp.concatenate([packed[3, t], qa], 0))
    mp = each(total_mobility, sp)
    tx = each(coefficient, kp, each(row_next, kp), mp, each(row_next, mp))
    ty = each(coefficient, kp, each(col_next, kp), mp, each(col_next, mp))
    tz = each(coefficient, kp, layer_next(kp), mp, layer_next(mp))
    tz = each(lambda c: vertical_ratio * c, tz)
    tz[-1] = jnp.where(lanes((SPAN, LANES)) < LANES - SEG, tz[-1], 0.0)
    terms = (tx, ty, tz)
    diag = each(lambda x, xp, y, yp, z, zp: storage_term + (z + zp) + (x + xp) + (y + yp), tx, each(row_prev, tx), ty, each(col_prev, ty), tz, layer_prev(tz))
    ip = each(lambda d: 1.0 / d, diag)
    flows_p = packed_flows(terms, pp)
    rp = each(lambda a, d: a - d, qp, packed_divergence(flows_p))
    zp0 = each(lambda a, b: a * b, rp, ip)
    flows_z = packed_flows(terms, zp0)
    gp = each(lambda a, d: storage_term * a + d, zp0, packed_divergence(flows_z))
    vp = each(lambda a, b, c: (a - b) * c, gp, rp, ip)
    flows_v = packed_flows(terms, vp)
    for t in range(TILES):
        s_pack[t], q_pack[t], cy_pack[t] = sp[t], qp[t], ty[t]
        for d in range(3):
            fp_pack[d, t], fz_pack[d, t], fv_pack[d, t] = flows_p[d][t], flows_z[d][t], flows_v[d][t]

    def first(z, carry):
        cz_prev, fz_prev = carry
        up = jnp.minimum(z + 1, NZ - 1)
        kz, pz, m = k[z], p[z], total_mobility(s[z])
        mx = row_next(m)
        ax = coefficient(kz, row_next(kz), m, mx)
        ay = edge_next(coefficient(kz, col_next(kz), m, col_next(m)), cy_pack, z)
        az = jnp.where(z < NZ - 1, vertical_ratio, 0.0) * coefficient(kz, k[up], m, total_mobility(s[up]))
        d = storage_term + (az + cz_prev) + (ax + row_prev(ax)) + (ay + edge_prev(ay, cy_pack, z))
        fx = ax * (pz - row_next(pz))
        fy = edge_next(ay * (pz - col_next(pz)), fp_pack.at[1], z)
        fzz = az * (pz - p[up])
        res = q[z] - ((fzz - fz_prev) + (fx - row_prev(fx)) + (fy - edge_prev(fy, fp_pack.at[1], z)))
        inverse = 1.0 / d
        cx[z], cy[z], cz[z], inv[z], r[z] = ax, ay, az, inverse, res
        fp[0, z], fp[1, z], fp[2, z] = fx, fy, fzz
        z0[z] = res * inverse
        return az, fzz

    zero = jnp.zeros((SPAN, LANES), F32)
    zero8 = jnp.zeros((ROWS, LANES), F32)
    lax.fori_loop(0, NZ, first, (zero, zero), unroll=NZ // 2)

    def second(z, carry):
        fz_prev, rz, zaz, rv, vaz = carry
        up = jnp.minimum(z + 1, NZ - 1)
        a = z0[z]
        fx = cx[z] * (a - row_next(a))
        fy = edge_next(cy[z] * (a - col_next(a)), fz_pack.at[1], z)
        fzz = cz[z] * (a - z0[up])
        g = storage_term * a + ((fzz - fz_prev) + (fx - row_prev(fx)) + (fy - edge_prev(fy, fz_pack.at[1], z)))
        fz[0, z], fz[1, z], fz[2, z] = fx, fy, fzz
        diff = g - r[z]
        b = diff * inv[z]
        v[z] = b
        a8, g8, d8, b8, r8 = a[:ROWS], g[:ROWS], diff[:ROWS], b[:ROWS], r[z, :ROWS]
        return fzz, rz + r8 * a8, zaz + a8 * g8, rv + a8 * d8, vaz + b8 * g8

    _, rz, zaz, rv, vaz = lax.fori_loop(0, NZ, second, (zero, zero8, zero8, zero8, zero8), unroll=NZ // 2)

    def third(z, carry):
        fz_prev, vav = carry
        up = jnp.minimum(z + 1, NZ - 1)
        a = v[z]
        fx = cx[z] * (a - row_next(a))
        fy = edge_next(cy[z] * (a - col_next(a)), fv_pack.at[1], z)
        fzz = cz[z] * (a - v[up])
        fv[0, z], fv[1, z], fv[2, z] = fx, fy, fzz
        w = storage_term * a + ((fzz - fz_prev) + (fx - row_prev(fx)) + (fy - edge_prev(fy, fv_pack.at[1], z)))
        return fzz, vav + a[:ROWS] * w[:ROWS]

    _, vav = lax.fori_loop(0, NZ, third, (zero, zero8), unroll=NZ // 2)
    row = zero8
    for i, x in enumerate((rz, zaz, rv, vaz, vav)):
        row = jnp.where(lanes() == i, jnp.sum(x), row)
    for i in range(sums.shape[0] // ROWS):
        sums[i * ROWS:(i + 1) * ROWS] = row


def finish(sums, p_own, z0, v, s, q, fp, fz, fv, s_pack, q_pack, fp_pack, fz_pack, fv_pack,
           pressure_out, s_out, flow, f1, s1, wy0_pack, wy1_pack, f0, pressure, s_new, sems):
    total = jnp.sum(sums[...], axis=0, keepdims=True)
    lane = lanes((1, LANES))
    rz, zaz, rv, vaz, vav = (jnp.sum(jnp.where(lane == i, total, 0.0), axis=1, keepdims=True) for i in range(5))
    ratio = vaz / zaz
    bottom = vav - ratio * vaz
    top = rv - ratio * rz
    good = bottom > 0.0
    b = jnp.where(good, top / jnp.where(good, bottom, 1.0), 0.0)
    a = rz / zaz - b * ratio
    a16, b16 = (jnp.broadcast_to(x, (SPAN, LANES)) for x in (a, b))

    def gained(rate, fraction):
        return jnp.maximum(rate, 0.0) + jnp.minimum(rate, 0.0) * fraction

    def upwind(flux, here, there):
        return flux * jnp.where(flux > 0.0, here, there)

    flows = [[fp_pack[d, t] + a16 * fz_pack[d, t] + b16 * fv_pack[d, t] for t in range(TILES)] for d in range(3)]
    s_now = [s_pack[t] for t in range(TILES)]
    q_now = [q_pack[t] for t in range(TILES)]
    for step, keep in enumerate((wy0_pack, wy1_pack)):
        fr = each(water_fraction, s_now)
        nexts = (each(row_next, fr), each(col_next, fr), layer_next(fr))
        water = [each(upwind, fl, fr, n) for fl, n in zip(flows, nexts)]
        for t in range(TILES):
            keep[t] = water[1][t]
        if step == 0:
            s_now = each(lambda x, rate, f, d: x + step_ratio * (gained(rate, f) - d), s_now, q_now, fr, packed_divergence(water))

    def fractions(z, c):
        f0[z] = water_fraction(s[z])
        return c

    lax.fori_loop(0, NZ, fractions, 0, unroll=NZ)

    def first(z, wz_prev):
        up = jnp.minimum(z + 1, NZ - 1)
        fx, fy, fzz = (fp[d, z] + a16 * fz[d, z] + b16 * fv[d, z] for d in range(3))
        flow[0, z], flow[1, z], flow[2, z] = fx, fy, fzz
        pressure[z] = p_own[z] + a16[:ROWS] * z0[z, :ROWS] + b16[:ROWS] * v[z, :ROWS]
        f = f0[z]
        wx = upwind(fx, f, row_next(f))
        wy = edge_next(upwind(fy, f, col_next(f)), wy0_pack, z)
        wz = upwind(fzz, f, f0[up])
        new = s[z] + step_ratio * (gained(q[z], f) - ((wz - wz_prev) + (wx - row_prev(wx)) + (wy - edge_prev(wy, wy0_pack, z))))
        s1[z] = new
        f1[z] = water_fraction(new)
        return wz

    lax.fori_loop(0, NZ, first, jnp.zeros((SPAN, LANES), F32), unroll=NZ)
    send = pltpu.make_async_copy(pressure, pressure_out, sems.at[0])
    send.start()

    def second(z, wz_prev):
        up = jnp.minimum(z + 1, NZ - 1)
        f = f1[z]
        wx = upwind(flow[0, z], f, row_next(f))
        wy = edge_next(upwind(flow[1, z], f, col_next(f)), wy1_pack, z)
        wz = upwind(flow[2, z, :ROWS], f[:ROWS], f1[up, :ROWS])
        east = (wy - edge_prev(wy, wy1_pack, z))[:ROWS]
        s_new[z] = s1[z, :ROWS] + step_ratio * (gained(q[z, :ROWS], f[:ROWS]) - ((wz - wz_prev) + (wx - row_prev(wx))[:ROWS] + east))
        return wz

    lax.fori_loop(0, NZ, second, jnp.zeros((ROWS, LANES), F32), unroll=NZ)
    send_s = pltpu.make_async_copy(s_new, s_out, sems.at[1])
    send_s.start()
    send.wait()
    send_s.wait()


VMEM = pl.BlockSpec(memory_space=pltpu.VMEM)
ANY = pl.BlockSpec(memory_space=pl.ANY)


def call(body, outs, args, scratch=()):
    args = [pltpu.with_memory_space_constraint(x, pltpu.VMEM) for x in args]
    return pl.pallas_call(
        body,
        name=body.__name__,
        out_shape=tuple(pltpu.VMEM(s, F32) for s in outs),
        in_specs=[VMEM] * len(args),
        out_specs=tuple(VMEM for _ in outs),
        scratch_shapes=[pltpu.VMEM(s, F32) for s in scratch],
    )(*args)


def ring(x, axis, by):
    n = lax.axis_size(axis)
    return lax.ppermute(x, axis, [(i, (i + by) % n) for i in range(n)])


def one_sample(k, s, p, q):
    own = (NZ, ROWS, LANES)
    assert k.shape == own
    cols = (TILES, ROWS, LANES)
    first, last, k, s, p, q = pl.pallas_call(
        pack_columns,
        name="pack_columns",
        out_shape=tuple(pltpu.VMEM(x, F32) for x in (cols, cols, own, own, own, own)),
        in_specs=[ANY] * 4,
        out_specs=(VMEM,) * 6,
        scratch_shapes=[pltpu.SemaphoreType.DMA((4,))],
    )(k, s, p, q)
    from_prev, from_next = ring(last, "gy", 1), ring(first, "gy", -1)
    message = (2 * NZ + 2 * TILES, ROWS, LANES)
    packed, to_prev, to_next = call(pack_rows, ((4,) + cols, message, message), (k, s, p, q, first, last, from_prev, from_next))
    prev, nxt = ring(to_next, "gx", 1), ring(to_prev, "gx", -1)
    size = lax.axis_size("gx") * lax.axis_size("gy")
    field, strip = (NZ, SPAN, LANES), (TILES, SPAN, LANES)
    mid = call(
        middle,
        ((size, LANES),) + (field,) * 4 + ((3,) + field,) * 3 + (strip,) * 2 + ((3,) + strip,) * 3,
        (k, s, p, q, packed, prev, nxt),
        (field,) * 7 + (strip,),
    )
    sums = lax.all_to_all(mid[0], ("gx", "gy"), 0, 0, tiled=True)
    args = [pltpu.with_memory_space_constraint(x, pltpu.VMEM) for x in (sums, p) + tuple(mid[1:])]
    return pl.pallas_call(
        finish,
        name="finish",
        out_shape=(jax.ShapeDtypeStruct(own, F32),) * 2,
        in_specs=[VMEM] * len(args),
        out_specs=(ANY, ANY),
        scratch_shapes=[pltpu.VMEM(x, F32) for x in ((3,) + field, field, field, strip, strip, field, own, own)] + [pltpu.SemaphoreType.DMA((2,))],
    )(*args)


def local(permeability, saturation, pressure_old, source):
    outs = [one_sample(permeability[i], saturation[i], pressure_old[i], source) for i in range(permeability.shape[0])]
    return jnp.stack([o[0] for o in outs]), jnp.stack([o[1] for o in outs])


def solution(mesh):
    field = P(None, None, "gx", "gy")
    return jax.shard_map(local, mesh=mesh, in_specs=(field, field, field, P(None, "gx", "gy")), out_specs=(field, field), check_vma=False)
```

```python
import jax
import jax.numpy as jnp
from jax import lax
from jax.experimental import pallas as pl
from jax.experimental.pallas import tpu as pltpu
from jax.sharding import PartitionSpec as P

storage_term = 0.5
vertical_ratio = 0.1
step_ratio = 0.05
water_viscosity = 1.0
oil_viscosity = 2.0

NZ, ROWS, LANES, HALO = 16, 8, 128, 4
SPAN = 2 * ROWS
SEG = 16
TILES = NZ * SEG // LANES
PER = LANES // SEG
F32 = jnp.float32


def lanes(shape=(ROWS, LANES)):
    return lax.broadcasted_iota(jnp.int32, shape, len(shape) - 1)


def sublanes(shape=(ROWS, LANES)):
    return lax.broadcasted_iota(jnp.int32, shape, len(shape) - 2)


def turn(x, by, axis):
    n = x.shape[axis]
    if isinstance(by, int):
        by %= n
        if by == 0:
            return x
    return pltpu.roll(x, by, axis)


def total_mobility(s):
    return s * s / water_viscosity + (1.0 - s) * (1.0 - s) / oil_viscosity


def water_fraction(s):
    return s * s / water_viscosity / total_mobility(s)


def coefficient(ka, kb, ma, mb):
    return ka * kb * (ma + mb) / jnp.maximum(ka + kb, 1e-30)


def row_next(x):
    return turn(x, -1, 0)


def row_prev(x):
    return turn(x, 1, 0)


def col_next(x):
    return turn(x, -1, 1)


def col_prev(x):
    return turn(x, 1, 1)


def pack_columns(k_in, s_in, p_in, q_in, to_prev, to_next, k, s, p, q, sems):
    copies = [pltpu.make_async_copy(a, b, sems.at[i]) for i, (a, b) in enumerate(((k_in, k), (s_in, s), (p_in, p), (q_in, q)))]
    for c in copies:
        c.start()
    seg = lanes() % SEG // 4
    layer = lanes() // SEG
    first = [jnp.zeros((ROWS, LANES), F32) for _ in range(TILES)]
    last = [jnp.zeros((ROWS, LANES), F32) for _ in range(TILES)]
    for i, ref in enumerate((k, s, p, q)):
        copies[i].wait()
        for t in range(TILES):
            for zz in range(PER):
                x = ref[t * PER + zz]
                here = (layer == zz) & (seg == i)
                at = zz * SEG + 4 * i
                first[t] = jnp.where(here, turn(x, at, 1), first[t])
                last[t] = jnp.where(here, turn(x, at + HALO, 1), last[t])
    for t in range(TILES):
        to_prev[t] = first[t]
        to_next[t] = last[t]


def pack_rows(k, s, p, q, own_first, own_last, from_prev, from_next, packed, to_prev, to_next):
    seg = lanes() % SEG // 4
    low = sublanes() < HALO

    even = lax.axis_index("gx") % 2 == 1

    def pair(at, a, b):
        before = jnp.where(low, a, turn(b, HALO, 0))
        after = jnp.where(low, turn(a, HALO, 0), b)
        to_prev[at] = jnp.where(even, after, before)
        to_next[at] = jnp.where(even, before, after)

    for t in range(TILES):
        cols = []
        for i in range(4):
            x = turn(from_prev[t], -4 * i, 1)
            x = jnp.where(seg == 1, turn(own_first[t], 4 - 4 * i, 1), x)
            x = jnp.where(seg == 2, turn(own_last[t], 8 - 4 * i, 1), x)
            x = jnp.where(seg == 3, turn(from_next[t], 12 - 4 * i, 1), x)
            packed[i, t] = x
            cols.append(x)
        pair(2 * NZ + t, cols[0], cols[1])
        pair(2 * NZ + TILES + t, cols[2], cols[3])

    for z in range(NZ):
        pair(z, k[z], s[z])
        pair(NZ + z, p[z], q[z])


def layer_next(x):
    edge = lanes((SPAN, LANES)) < LANES - SEG
    moved = [turn(t, -SEG, 1) for t in x]
    return [jnp.where(edge, moved[i], moved[(i + 1) % TILES]) for i in range(TILES)]


def layer_prev(x):
    edge = lanes((SPAN, LANES)) >= SEG
    moved = [turn(t, SEG, 1) for t in x]
    return [jnp.where(edge, moved[i], moved[(i - 1) % TILES]) for i in range(TILES)]


def each(f, *args):
    return [f(*a) for a in zip(*args)]


def packed_divergence(flows):
    fx, fy, fz = flows
    return each(lambda x, xp, y, yp, z, zp: (z - zp) + (x - xp) + (y - yp), fx, each(row_prev, fx), fy, each(col_prev, fy), fz, layer_prev(fz))


def packed_flows(terms, v):
    nexts = (each(row_next, v), each(col_next, v), layer_next(v))
    return [each(lambda c, a, b: c * (a - b), term, v, n) for term, n in zip(terms, nexts)]


def edge_next(y, packed_face, z):
    at = LANES - 1 - (z % PER * SEG + 11)
    return jnp.where(lanes((SPAN, LANES)) == LANES - 1, pltpu.roll(packed_face[z // PER], at, 1), y)


def edge_prev(y, packed_face, z):
    at = LANES - (z % PER * SEG + 3)
    return jnp.where(lanes((SPAN, LANES)) == 0, pltpu.roll(packed_face[z // PER], at, 1), col_prev(y))


def middle(k_own, s_own, p_own, q_own, packed, prev, nxt,
           sums, z0, v, s, q, fp, fz, fv, s_pack, q_pack, fp_pack, fz_pack, fv_pack,
           k, p, cx, cy, cz, inv, r, cy_pack):
    gx, gy = lax.axis_index("gx"), lax.axis_index("gy")
    last_gx, last_gy = lax.axis_size("gx") - 1, lax.axis_size("gy") - 1
    row8 = sublanes()
    low = row8 < HALO
    inside_rows = jnp.where(low, jnp.where(gx == last_gx, 0.0, 1.0), jnp.where(gx == 0, 0.0, 1.0))
    seg8 = lanes() % SEG // 4
    inside_cols = jnp.where(seg8 == 0, jnp.where(gy == 0, 0.0, 1.0), jnp.where(seg8 == 3, jnp.where(gy == last_gy, 0.0, 1.0), 1.0))

    even = gx % 2 == 1

    def halo_rows(at):
        below, above = jnp.where(even, prev[at], nxt[at]), jnp.where(even, nxt[at], prev[at])
        return jnp.where(low, below, turn(above, HALO, 0)), jnp.where(low, turn(below, HALO, 0), above)

    def assemble(z, _):
        ka, sa = halo_rows(z)
        pa, qa = halo_rows(NZ + z)
        k[z, :ROWS], k[z, ROWS:] = k_own[z], ka * inside_rows
        s[z, :ROWS], s[z, ROWS:] = s_own[z], sa
        p[z, :ROWS], p[z, ROWS:] = p_own[z], pa
        q[z, :ROWS], q[z, ROWS:] = q_own[z], qa
        return _

    lax.fori_loop(0, NZ, assemble, 0, unroll=NZ // 2)

    kp, sp, pp, qp = [], [], [], []
    for t in range(TILES):
        ka, sa = halo_rows(2 * NZ + t)
        pa, qa = halo_rows(2 * NZ + TILES + t)
        kp.append(jnp.concatenate([packed[0, t] * inside_cols, ka * inside_rows * inside_cols], 0))
        sp.append(jnp.concatenate([packed[1, t], sa], 0))
        pp.append(jnp.concatenate([packed[2, t], pa], 0))
        qp.append(jnp.concatenate([packed[3, t], qa], 0))
    mp = each(total_mobility, sp)
    tx = each(coefficient, kp, each(row_next, kp), mp, each(row_next, mp))
    ty = each(coefficient, kp, each(col_next, kp), mp, each(col_next, mp))
    tz = each(coefficient, kp, layer_next(kp), mp, layer_next(mp))
    tz = each(lambda c: vertical_ratio * c, tz)
    tz[-1] = jnp.where(lanes((SPAN, LANES)) < LANES - SEG, tz[-1], 0.0)
    terms = (tx, ty, tz)
    diag = each(lambda x, xp, y, yp, z, zp: storage_term + (z + zp) + (x + xp) + (y + yp), tx, each(row_prev, tx), ty, each(col_prev, ty), tz, layer_prev(tz))
    ip = each(lambda d: 1.0 / d, diag)
    flows_p = packed_flows(terms, pp)
    rp = each(lambda a, d: a - d, qp, packed_divergence(flows_p))
    zp0 = each(lambda a, b: a * b, rp, ip)
    flows_z = packed_flows(terms, zp0)
    gp = each(lambda a, d: storage_term * a + d, zp0, packed_divergence(flows_z))
    vp = each(lambda a, b, c: (a - b) * c, gp, rp, ip)
    flows_v = packed_flows(terms, vp)
    for t in range(TILES):
        s_pack[t], q_pack[t], cy_pack[t] = sp[t], qp[t], ty[t]
        for d in range(3):
            fp_pack[d, t], fz_pack[d, t], fv_pack[d, t] = flows_p[d][t], flows_z[d][t], flows_v[d][t]

    def first(z, carry):
        cz_prev, fz_prev = carry
        up = jnp.minimum(z + 1, NZ - 1)
        kz, pz, m = k[z], p[z], total_mobility(s[z])
        mx = row_next(m)
        ax = coefficient(kz, row_next(kz), m, mx)
        ay = edge_next(coefficient(kz, col_next(kz), m, col_next(m)), cy_pack, z)
        az = jnp.where(z < NZ - 1, vertical_ratio, 0.0) * coefficient(kz, k[up], m, total_mobility(s[up]))
        d = storage_term + (az + cz_prev) + (ax + row_prev(ax)) + (ay + edge_prev(ay, cy_pack, z))
        fx = ax * (pz - row_next(pz))
        fy = edge_next(ay * (pz - col_next(pz)), fp_pack.at[1], z)
        fzz = az * (pz - p[up])
        res = q[z] - ((fzz - fz_prev) + (fx - row_prev(fx)) + (fy - edge_prev(fy, fp_pack.at[1], z)))
        inverse = 1.0 / d
        cx[z], cy[z], cz[z], inv[z], r[z] = ax, ay, az, inverse, res
        fp[0, z], fp[1, z], fp[2, z] = fx, fy, fzz
        z0[z] = res * inverse
        return az, fzz

    zero = jnp.zeros((SPAN, LANES), F32)
    zero8 = jnp.zeros((ROWS, LANES), F32)
    lax.fori_loop(0, NZ, first, (zero, zero), unroll=NZ // 2)

    def second(z, carry):
        fz_prev, rz, zaz, rv, vaz = carry
        up = jnp.minimum(z + 1, NZ - 1)
        a = z0[z]
        fx = cx[z] * (a - row_next(a))
        fy = edge_next(cy[z] * (a - col_next(a)), fz_pack.at[1], z)
        fzz = cz[z] * (a - z0[up])
        g = storage_term * a + ((fzz - fz_prev) + (fx - row_prev(fx)) + (fy - edge_prev(fy, fz_pack.at[1], z)))
        fz[0, z], fz[1, z], fz[2, z] = fx, fy, fzz
        diff = g - r[z]
        b = diff * inv[z]
        v[z] = b
        a8, g8, d8, b8, r8 = a[:ROWS], g[:ROWS], diff[:ROWS], b[:ROWS], r[z, :ROWS]
        return fzz, rz + r8 * a8, zaz + a8 * g8, rv + a8 * d8, vaz + b8 * g8

    _, rz, zaz, rv, vaz = lax.fori_loop(0, NZ, second, (zero, zero8, zero8, zero8, zero8), unroll=NZ)

    def third(z, carry):
        fz_prev, vav = carry
        up = jnp.minimum(z + 1, NZ - 1)
        a = v[z]
        fx = cx[z] * (a - row_next(a))
        fy = edge_next(cy[z] * (a - col_next(a)), fv_pack.at[1], z)
        fzz = cz[z] * (a - v[up])
        fv[0, z], fv[1, z], fv[2, z] = fx, fy, fzz
        w = storage_term * a + ((fzz - fz_prev) + (fx - row_prev(fx)) + (fy - edge_prev(fy, fv_pack.at[1], z)))
        return fzz, vav + a[:ROWS] * w[:ROWS]

    _, vav = lax.fori_loop(0, NZ, third, (zero, zero8), unroll=NZ)
    row = zero8
    for i, x in enumerate((rz, zaz, rv, vaz, vav)):
        row = jnp.where(lanes() == i, jnp.sum(x), row)
    for i in range(sums.shape[0] // ROWS):
        sums[i * ROWS:(i + 1) * ROWS] = row


def finish(sums, p_own, z0, v, s, q, fp, fz, fv, s_pack, q_pack, fp_pack, fz_pack, fv_pack,
           pressure_out, s_out, flow, f1, s1, wy0_pack, wy1_pack, f0, pressure, s_new, sems):
    total = jnp.sum(sums[...], axis=0, keepdims=True)
    lane = lanes((1, LANES))
    rz, zaz, rv, vaz, vav = (jnp.sum(jnp.where(lane == i, total, 0.0), axis=1, keepdims=True) for i in range(5))
    ratio = vaz / zaz
    bottom = vav - ratio * vaz
    top = rv - ratio * rz
    good = bottom > 0.0
    b = jnp.where(good, top / jnp.where(good, bottom, 1.0), 0.0)
    a = rz / zaz - b * ratio
    a16, b16 = (jnp.broadcast_to(x, (SPAN, LANES)) for x in (a, b))

    def gained(rate, fraction):
        return jnp.maximum(rate, 0.0) + jnp.minimum(rate, 0.0) * fraction

    def upwind(flux, here, there):
        return flux * jnp.where(flux > 0.0, here, there)

    flows = [[fp_pack[d, t] + a16 * fz_pack[d, t] + b16 * fv_pack[d, t] for t in range(TILES)] for d in range(3)]
    s_now = [s_pack[t] for t in range(TILES)]
    q_now = [q_pack[t] for t in range(TILES)]
    for step, keep in enumerate((wy0_pack, wy1_pack)):
        fr = each(water_fraction, s_now)
        nexts = (each(row_next, fr), each(col_next, fr), layer_next(fr))
        water = [each(upwind, fl, fr, n) for fl, n in zip(flows, nexts)]
        for t in range(TILES):
            keep[t] = water[1][t]
        if step == 0:
            s_now = each(lambda x, rate, f, d: x + step_ratio * (gained(rate, f) - d), s_now, q_now, fr, packed_divergence(water))

    def fractions(z, c):
        f0[z] = water_fraction(s[z])
        return c

    lax.fori_loop(0, NZ, fractions, 0, unroll=NZ)

    def first(z, wz_prev):
        up = jnp.minimum(z + 1, NZ - 1)
        fx, fy, fzz = (fp[d, z] + a16 * fz[d, z] + b16 * fv[d, z] for d in range(3))
        flow[0, z], flow[1, z], flow[2, z] = fx, fy, fzz
        pressure[z] = p_own[z] + a16[:ROWS] * z0[z, :ROWS] + b16[:ROWS] * v[z, :ROWS]
        f = f0[z]
        wx = upwind(fx, f, row_next(f))
        wy = edge_next(upwind(fy, f, col_next(f)), wy0_pack, z)
        wz = upwind(fzz, f, f0[up])
        new = s[z] + step_ratio * (gained(q[z], f) - ((wz - wz_prev) + (wx - row_prev(wx)) + (wy - edge_prev(wy, wy0_pack, z))))
        s1[z] = new
        f1[z] = water_fraction(new)
        return wz

    lax.fori_loop(0, NZ, first, jnp.zeros((SPAN, LANES), F32), unroll=NZ)
    send = pltpu.make_async_copy(pressure, pressure_out, sems.at[0])
    send.start()

    def second(z, wz_prev):
        up = jnp.minimum(z + 1, NZ - 1)
        f = f1[z]
        wx = upwind(flow[0, z], f, row_next(f))
        wy = edge_next(upwind(flow[1, z], f, col_next(f)), wy1_pack, z)
        wz = upwind(flow[2, z, :ROWS], f[:ROWS], f1[up, :ROWS])
        east = (wy - edge_prev(wy, wy1_pack, z))[:ROWS]
        s_new[z] = s1[z, :ROWS] + step_ratio * (gained(q[z, :ROWS], f[:ROWS]) - ((wz - wz_prev) + (wx - row_prev(wx))[:ROWS] + east))
        return wz

    lax.fori_loop(0, NZ, second, jnp.zeros((ROWS, LANES), F32), unroll=NZ)
    send_s = pltpu.make_async_copy(s_new, s_out, sems.at[1])
    send_s.start()
    send.wait()
    send_s.wait()


VMEM = pl.BlockSpec(memory_space=pltpu.VMEM)
ANY = pl.BlockSpec(memory_space=pl.ANY)


def call(body, outs, args, scratch=()):
    args = [pltpu.with_memory_space_constraint(x, pltpu.VMEM) for x in args]
    return pl.pallas_call(
        body,
        name=body.__name__,
        out_shape=tuple(pltpu.VMEM(s, F32) for s in outs),
        in_specs=[VMEM] * len(args),
        out_specs=tuple(VMEM for _ in outs),
        scratch_shapes=[pltpu.VMEM(s, F32) for s in scratch],
    )(*args)


def ring(x, axis, by):
    n = lax.axis_size(axis)
    return lax.ppermute(x, axis, [(i, (i + by) % n) for i in range(n)])


def trade(x, first):
    nx, ny = lax.axis_size("gx"), lax.axis_size("gy")
    other = {}
    for i in range(first, nx - 1, 2):
        other[i], other[i + 1] = i + 1, i
    pairs = [(i * ny + j, other[i] * ny + j if i in other else i * ny + (j ^ 1)) for i in range(nx) for j in range(ny)]
    return lax.ppermute(x, ("gx", "gy"), pairs)


def one_sample(k, s, p, q):
    own = (NZ, ROWS, LANES)
    assert k.shape == own
    cols = (TILES, ROWS, LANES)
    first, last, k, s, p, q = pl.pallas_call(
        pack_columns,
        name="pack_columns",
        out_shape=tuple(pltpu.VMEM(x, F32) for x in (cols, cols, own, own, own, own)),
        in_specs=[ANY] * 4,
        out_specs=(VMEM,) * 6,
        scratch_shapes=[pltpu.SemaphoreType.DMA((4,))],
    )(k, s, p, q)
    from_prev, from_next = ring(last, "gy", 1), ring(first, "gy", -1)
    message = (2 * NZ + 2 * TILES, ROWS, LANES)
    packed, to_prev, to_next = call(pack_rows, ((4,) + cols, message, message), (k, s, p, q, first, last, from_prev, from_next))
    prev, nxt = trade(to_prev, 1), trade(to_next, 0)
    size = lax.axis_size("gx") * lax.axis_size("gy")
    field, strip = (NZ, SPAN, LANES), (TILES, SPAN, LANES)
    mid = call(
        middle,
        ((size, LANES),) + (field,) * 4 + ((3,) + field,) * 3 + (strip,) * 2 + ((3,) + strip,) * 3,
        (k, s, p, q, packed, prev, nxt),
        (field,) * 7 + (strip,),
    )
    sums = lax.all_to_all(mid[0], ("gx", "gy"), 0, 0, tiled=True)
    args = [pltpu.with_memory_space_constraint(x, pltpu.VMEM) for x in (sums, p) + tuple(mid[1:])]
    return pl.pallas_call(
        finish,
        name="finish",
        out_shape=(jax.ShapeDtypeStruct(own, F32),) * 2,
        in_specs=[VMEM] * len(args),
        out_specs=(ANY, ANY),
        scratch_shapes=[pltpu.VMEM(x, F32) for x in ((3,) + field, field, field, strip, strip, field, own, own)] + [pltpu.SemaphoreType.DMA((2,))],
    )(*args)


def local(permeability, saturation, pressure_old, source):
    outs = [one_sample(permeability[i], saturation[i], pressure_old[i], source) for i in range(permeability.shape[0])]
    return jnp.stack([o[0] for o in outs]), jnp.stack([o[1] for o in outs])


def solution(mesh):
    field = P(None, None, "gx", "gy")
    return jax.shard_map(local, mesh=mesh, in_specs=(field, field, field, P(None, "gx", "gy")), out_specs=(field, field), check_vma=False)
```

```python
import jax
import jax.numpy as jnp
from jax import lax
from jax.experimental import pallas as pl
from jax.experimental.pallas import tpu as pltpu
from jax.sharding import PartitionSpec as P


storage_term = 0.5
vertical_ratio = 0.1
step_ratio = 0.05
water_viscosity = 1.0
oil_viscosity = 2.0

NZ, ROWS, LANES, HALO = 16, 8, 128, 4
SPAN = 2 * ROWS
SEG = 16
TILES = NZ * SEG // LANES
PER = LANES // SEG
F32 = jnp.float32


def lanes(shape=(ROWS, LANES)):
    return lax.broadcasted_iota(jnp.int32, shape, len(shape) - 1)


def sublanes(shape=(ROWS, LANES)):
    return lax.broadcasted_iota(jnp.int32, shape, len(shape) - 2)


def turn(x, by, axis):
    n = x.shape[axis]
    if isinstance(by, int):
        by %= n
        if by == 0:
            return x
    return pltpu.roll(x, by, axis)


def total_mobility(s):
    return s * s / water_viscosity + (1.0 - s) * (1.0 - s) / oil_viscosity


def water_fraction(s):
    return s * s / water_viscosity / total_mobility(s)


def coefficient(ka, kb, ma, mb):
    return ka * kb * (ma + mb) / jnp.maximum(ka + kb, 1e-30)


def row_next(x):
    return turn(x, -1, 0)


def row_prev(x):
    return turn(x, 1, 0)


def col_next(x):
    return turn(x, -1, 1)


def col_prev(x):
    return turn(x, 1, 1)


def pack_columns(k_in, s_in, p_in, q_in, to_prev, to_next, k, s, p, q, sems):
    copies = [pltpu.make_async_copy(a, b, sems.at[i]) for i, (a, b) in enumerate(((k_in, k), (s_in, s), (p_in, p), (q_in, q)))]
    for c in copies:
        c.start()
    seg = lanes() % SEG // 4
    layer = lanes() // SEG
    first = [jnp.zeros((ROWS, LANES), F32) for _ in range(TILES)]
    last = [jnp.zeros((ROWS, LANES), F32) for _ in range(TILES)]
    for i, ref in enumerate((k, s, p, q)):
        copies[i].wait()
        for t in range(TILES):
            for zz in range(PER):
                x = ref[t * PER + zz]
                here = (layer == zz) & (seg == i)
                at = zz * SEG + 4 * i
                first[t] = jnp.where(here, turn(x, at, 1), first[t])
                last[t] = jnp.where(here, turn(x, at + HALO, 1), last[t])
    for t in range(TILES):
        to_prev[t] = first[t]
        to_next[t] = last[t]


def pair(at, a, b, to_far, to_near):
    odd = lax.axis_index("gx") % 2 == 1
    low = sublanes() < HALO
    before = jnp.where(low, a, turn(b, HALO, 0))
    after = jnp.where(low, turn(a, HALO, 0), b)
    to_far[at] = jnp.where(odd, after, before)
    to_near[at] = jnp.where(odd, before, after)


def pack_body(k, s, p, q, to_far, to_near):
    for z in range(NZ):
        pair(z, k[z], s[z], to_far, to_near)
        pair(NZ + z, p[z], q[z], to_far, to_near)


def pack_strip(own_first, own_last, from_prev, from_next, packed, to_far, to_near):
    seg = lanes() % SEG // 4
    for t in range(TILES):
        cols = []
        for i in range(4):
            x = turn(from_prev[t], -4 * i, 1)
            x = jnp.where(seg == 1, turn(own_first[t], 4 - 4 * i, 1), x)
            x = jnp.where(seg == 2, turn(own_last[t], 8 - 4 * i, 1), x)
            x = jnp.where(seg == 3, turn(from_next[t], 12 - 4 * i, 1), x)
            packed[i, t] = x
            cols.append(x)
        pair(t, cols[0], cols[1], to_far, to_near)
        pair(TILES + t, cols[2], cols[3], to_far, to_near)


def layer_next(x):
    edge = lanes((SPAN, LANES)) < LANES - SEG
    moved = [turn(t, -SEG, 1) for t in x]
    return [jnp.where(edge, moved[i], moved[(i + 1) % TILES]) for i in range(TILES)]


def layer_prev(x):
    edge = lanes((SPAN, LANES)) >= SEG
    moved = [turn(t, SEG, 1) for t in x]
    return [jnp.where(edge, moved[i], moved[(i - 1) % TILES]) for i in range(TILES)]


def each(f, *args):
    return [f(*a) for a in zip(*args)]


def packed_divergence(flows):
    fx, fy, fz = flows
    return each(lambda x, xp, y, yp, z, zp: (z - zp) + (x - xp) + (y - yp), fx, each(row_prev, fx), fy, each(col_prev, fy), fz, layer_prev(fz))


def packed_flows(terms, v):
    nexts = (each(row_next, v), each(col_next, v), layer_next(v))
    return [each(lambda c, a, b: c * (a - b), term, v, n) for term, n in zip(terms, nexts)]


def edge_next(y, packed_face, z):
    at = LANES - 1 - (z % PER * SEG + 11)
    return jnp.where(lanes((SPAN, LANES)) == LANES - 1, pltpu.roll(packed_face[z // PER], at, 1), y)


def edge_prev(y, packed_face, z):
    at = LANES - (z % PER * SEG + 3)
    return jnp.where(lanes((SPAN, LANES)) == 0, pltpu.roll(packed_face[z // PER], at, 1), col_prev(y))


def middle(k_own, s_own, p_own, q_own, packed, far, near, far_strip, near_strip,
           sums, z0, v, s, q, fp, fz, fv, s_pack, q_pack, fp_pack, fz_pack, fv_pack,
           k, p, cx, cy, cz, inv, r, cy_pack):
    gx, gy = lax.axis_index("gx"), lax.axis_index("gy")
    last_gx, last_gy = lax.axis_size("gx") - 1, lax.axis_size("gy") - 1
    row8 = sublanes()
    low = row8 < HALO
    inside_rows = jnp.where(low, jnp.where(gx == last_gx, 0.0, 1.0), jnp.where(gx == 0, 0.0, 1.0))
    seg8 = lanes() % SEG // 4
    inside_cols = jnp.where(seg8 == 0, jnp.where(gy == 0, 0.0, 1.0), jnp.where(seg8 == 3, jnp.where(gy == last_gy, 0.0, 1.0), 1.0))

    odd = gx % 2 == 1

    def halo_rows(at, far, near):
        below, above = jnp.where(odd, far[at], near[at]), jnp.where(odd, near[at], far[at])
        return jnp.where(low, below, turn(above, HALO, 0)), jnp.where(low, turn(below, HALO, 0), above)

    def assemble(z, _):
        ka, sa = halo_rows(z, far, near)
        pa, qa = halo_rows(NZ + z, far, near)
        k[z, :ROWS], k[z, ROWS:] = k_own[z], ka * inside_rows
        s[z, :ROWS], s[z, ROWS:] = s_own[z], sa
        p[z, :ROWS], p[z, ROWS:] = p_own[z], pa
        q[z, :ROWS], q[z, ROWS:] = q_own[z], qa
        return _

    lax.fori_loop(0, NZ, assemble, 0, unroll=NZ // 2)

    kp, sp, pp, qp = [], [], [], []
    for t in range(TILES):
        ka, sa = halo_rows(t, far_strip, near_strip)
        pa, qa = halo_rows(TILES + t, far_strip, near_strip)
        kp.append(jnp.concatenate([packed[0, t] * inside_cols, ka * inside_rows * inside_cols], 0))
        sp.append(jnp.concatenate([packed[1, t], sa], 0))
        pp.append(jnp.concatenate([packed[2, t], pa], 0))
        qp.append(jnp.concatenate([packed[3, t], qa], 0))
    mp = each(total_mobility, sp)
    tx = each(coefficient, kp, each(row_next, kp), mp, each(row_next, mp))
    ty = each(coefficient, kp, each(col_next, kp), mp, each(col_next, mp))
    tz = each(coefficient, kp, layer_next(kp), mp, layer_next(mp))
    tz = each(lambda c: vertical_ratio * c, tz)
    tz[-1] = jnp.where(lanes((SPAN, LANES)) < LANES - SEG, tz[-1], 0.0)
    terms = (tx, ty, tz)
    diag = each(lambda x, xp, y, yp, z, zp: storage_term + (z + zp) + (x + xp) + (y + yp), tx, each(row_prev, tx), ty, each(col_prev, ty), tz, layer_prev(tz))
    ip = each(lambda d: 1.0 / d, diag)
    flows_p = packed_flows(terms, pp)
    rp = each(lambda a, d: a - d, qp, packed_divergence(flows_p))
    zp0 = each(lambda a, b: a * b, rp, ip)
    flows_z = packed_flows(terms, zp0)
    gp = each(lambda a, d: storage_term * a + d, zp0, packed_divergence(flows_z))
    vp = each(lambda a, b, c: (a - b) * c, gp, rp, ip)
    flows_v = packed_flows(terms, vp)
    for t in range(TILES):
        s_pack[t], q_pack[t], cy_pack[t] = sp[t], qp[t], ty[t]
        for d in range(3):
            fp_pack[d, t], fz_pack[d, t], fv_pack[d, t] = flows_p[d][t], flows_z[d][t], flows_v[d][t]

    def first(z, carry):
        cz_prev, fz_prev = carry
        up = jnp.minimum(z + 1, NZ - 1)
        kz, pz, m = k[z], p[z], total_mobility(s[z])
        mx = row_next(m)
        ax = coefficient(kz, row_next(kz), m, mx)
        ay = edge_next(coefficient(kz, col_next(kz), m, col_next(m)), cy_pack, z)
        az = jnp.where(z < NZ - 1, vertical_ratio, 0.0) * coefficient(kz, k[up], m, total_mobility(s[up]))
        d = storage_term + (az + cz_prev) + (ax + row_prev(ax)) + (ay + edge_prev(ay, cy_pack, z))
        fx = ax * (pz - row_next(pz))
        fy = edge_next(ay * (pz - col_next(pz)), fp_pack.at[1], z)
        fzz = az * (pz - p[up])
        res = q[z] - ((fzz - fz_prev) + (fx - row_prev(fx)) + (fy - edge_prev(fy, fp_pack.at[1], z)))
        inverse = 1.0 / d
        cx[z], cy[z], cz[z], inv[z], r[z] = ax, ay, az, inverse, res
        fp[0, z], fp[1, z], fp[2, z] = fx, fy, fzz
        z0[z] = res * inverse
        return az, fzz

    zero = jnp.zeros((SPAN, LANES), F32)
    zero8 = jnp.zeros((ROWS, LANES), F32)
    lax.fori_loop(0, NZ, first, (zero, zero), unroll=NZ // 2)

    def second(z, carry):
        fz_prev, rz, zaz, rv, vaz = carry
        up = jnp.minimum(z + 1, NZ - 1)
        a = z0[z]
        fx = cx[z] * (a - row_next(a))
        fy = edge_next(cy[z] * (a - col_next(a)), fz_pack.at[1], z)
        fzz = cz[z] * (a - z0[up])
        g = storage_term * a + ((fzz - fz_prev) + (fx - row_prev(fx)) + (fy - edge_prev(fy, fz_pack.at[1], z)))
        fz[0, z], fz[1, z], fz[2, z] = fx, fy, fzz
        diff = g - r[z]
        b = diff * inv[z]
        v[z] = b
        a8, g8, d8, b8, r8 = a[:ROWS], g[:ROWS], diff[:ROWS], b[:ROWS], r[z, :ROWS]
        return fzz, rz + r8 * a8, zaz + a8 * g8, rv + a8 * d8, vaz + b8 * g8

    _, rz, zaz, rv, vaz = lax.fori_loop(0, NZ, second, (zero, zero8, zero8, zero8, zero8), unroll=NZ)

    def third(z, carry):
        fz_prev, vav = carry
        up = jnp.minimum(z + 1, NZ - 1)
        a = v[z]
        fx = cx[z] * (a - row_next(a))
        fy = edge_next(cy[z] * (a - col_next(a)), fv_pack.at[1], z)
        fzz = cz[z] * (a - v[up])
        fv[0, z], fv[1, z], fv[2, z] = fx, fy, fzz
        w = storage_term * a + ((fzz - fz_prev) + (fx - row_prev(fx)) + (fy - edge_prev(fy, fv_pack.at[1], z)))
        return fzz, vav + a[:ROWS] * w[:ROWS]

    _, vav = lax.fori_loop(0, NZ, third, (zero, zero8), unroll=NZ)
    row = zero8
    for i, x in enumerate((rz, zaz, rv, vaz, vav)):
        row = jnp.where(lanes() == i, jnp.sum(x), row)
    for i in range(sums.shape[0] // ROWS):
        sums[i * ROWS:(i + 1) * ROWS] = row


def finish(sums, p_own, z0, v, s, q, fp, fz, fv, s_pack, q_pack, fp_pack, fz_pack, fv_pack,
           pressure_out, s_out, flow, f1, s1, wy0_pack, wy1_pack, f0, pressure, s_new, sems):
    total = jnp.sum(sums[...], axis=0, keepdims=True)
    lane = lanes((1, LANES))
    rz, zaz, rv, vaz, vav = (jnp.sum(jnp.where(lane == i, total, 0.0), axis=1, keepdims=True) for i in range(5))
    ratio = vaz / zaz
    bottom = vav - ratio * vaz
    top = rv - ratio * rz
    good = bottom > 0.0
    b = jnp.where(good, top / jnp.where(good, bottom, 1.0), 0.0)
    a = rz / zaz - b * ratio
    a16, b16 = (jnp.broadcast_to(x, (SPAN, LANES)) for x in (a, b))

    def gained(rate, fraction):
        return jnp.maximum(rate, 0.0) + jnp.minimum(rate, 0.0) * fraction

    def upwind(flux, here, there):
        return flux * jnp.where(flux > 0.0, here, there)

    flows = [[fp_pack[d, t] + a16 * fz_pack[d, t] + b16 * fv_pack[d, t] for t in range(TILES)] for d in range(3)]
    s_now = [s_pack[t] for t in range(TILES)]
    q_now = [q_pack[t] for t in range(TILES)]
    for step, keep in enumerate((wy0_pack, wy1_pack)):
        fr = each(water_fraction, s_now)
        nexts = (each(row_next, fr), each(col_next, fr), layer_next(fr))
        water = [each(upwind, fl, fr, n) for fl, n in zip(flows, nexts)]
        for t in range(TILES):
            keep[t] = water[1][t]
        if step == 0:
            s_now = each(lambda x, rate, f, d: x + step_ratio * (gained(rate, f) - d), s_now, q_now, fr, packed_divergence(water))

    def fractions(z, c):
        f0[z] = water_fraction(s[z])
        return c

    lax.fori_loop(0, NZ, fractions, 0, unroll=NZ)

    def first(z, wz_prev):
        up = jnp.minimum(z + 1, NZ - 1)
        fx, fy, fzz = (fp[d, z] + a16 * fz[d, z] + b16 * fv[d, z] for d in range(3))
        flow[0, z], flow[1, z], flow[2, z] = fx, fy, fzz
        pressure[z] = p_own[z] + a16[:ROWS] * z0[z, :ROWS] + b16[:ROWS] * v[z, :ROWS]
        f = f0[z]
        wx = upwind(fx, f, row_next(f))
        wy = edge_next(upwind(fy, f, col_next(f)), wy0_pack, z)
        wz = upwind(fzz, f, f0[up])
        new = s[z] + step_ratio * (gained(q[z], f) - ((wz - wz_prev) + (wx - row_prev(wx)) + (wy - edge_prev(wy, wy0_pack, z))))
        s1[z] = new
        f1[z] = water_fraction(new)
        return wz

    lax.fori_loop(0, NZ, first, jnp.zeros((SPAN, LANES), F32), unroll=NZ)
    send = pltpu.make_async_copy(pressure, pressure_out, sems.at[0])
    send.start()

    def second(z, wz_prev):
        up = jnp.minimum(z + 1, NZ - 1)
        f = f1[z]
        wx = upwind(flow[0, z], f, row_next(f))
        wy = edge_next(upwind(flow[1, z], f, col_next(f)), wy1_pack, z)
        wz = upwind(flow[2, z, :ROWS], f[:ROWS], f1[up, :ROWS])
        east = (wy - edge_prev(wy, wy1_pack, z))[:ROWS]
        s_new[z] = s1[z, :ROWS] + step_ratio * (gained(q[z, :ROWS], f[:ROWS]) - ((wz - wz_prev) + (wx - row_prev(wx))[:ROWS] + east))
        return wz

    lax.fori_loop(0, NZ, second, jnp.zeros((ROWS, LANES), F32), unroll=NZ)
    send_s = pltpu.make_async_copy(s_new, s_out, sems.at[1])
    send_s.start()
    send.wait()
    send_s.wait()


VMEM = pl.BlockSpec(memory_space=pltpu.VMEM)
ANY = pl.BlockSpec(memory_space=pl.ANY)


def call(body, outs, args, scratch=()):
    args = [pltpu.with_memory_space_constraint(x, pltpu.VMEM) for x in args]
    return pl.pallas_call(
        body,
        out_shape=tuple(pltpu.VMEM(s, F32) for s in outs),
        in_specs=[VMEM] * len(args),
        out_specs=tuple(VMEM for _ in outs),
        scratch_shapes=[pltpu.VMEM(s, F32) for s in scratch],
    )(*args)


def ring(x, axis, by):
    n = lax.axis_size(axis)
    return lax.ppermute(x, axis, [(i, (i + by) % n) for i in range(n)])


def trade(x, first):
    nx, ny = lax.axis_size("gx"), lax.axis_size("gy")
    other = {}
    for i in range(first, nx - 1, 2):
        other[i], other[i + 1] = i + 1, i
    pairs = [(i * ny + j, other[i] * ny + j if i in other else i * ny + (j ^ 1)) for i in range(nx) for j in range(ny)]
    return lax.ppermute(x, ("gx", "gy"), pairs)


def one_sample(k, s, p, q):
    own = (NZ, ROWS, LANES)
    assert k.shape == own
    cols = (TILES, ROWS, LANES)
    first, last, k, s, p, q = pl.pallas_call(
        pack_columns,
        name="pack_columns",
        out_shape=tuple(pltpu.VMEM(x, F32) for x in (cols, cols, own, own, own, own)),
        in_specs=[ANY] * 4,
        out_specs=(VMEM,) * 6,
        scratch_shapes=[pltpu.SemaphoreType.DMA((4,))],
    )(k, s, p, q)
    from_prev = ring(last, "gy", 1)
    from_next = ring(first, "gy", -1)
    body, strips = (2 * NZ, ROWS, LANES), (2 * TILES, ROWS, LANES)
    to_far, to_near = call(pack_body, (body, body), (k, s, p, q))
    far = trade(to_far, 1)
    near = trade(to_near, 0)
    packed, to_far, to_near = call(pack_strip, ((4,) + cols, strips, strips), (first, last, from_prev, from_next))
    far_strip, near_strip = trade(to_far, 1), trade(to_near, 0)
    size = lax.axis_size("gx") * lax.axis_size("gy")
    field, strip = (NZ, SPAN, LANES), (TILES, SPAN, LANES)
    mid = call(
        middle,
        ((size, LANES),) + (field,) * 4 + ((3,) + field,) * 3 + (strip,) * 2 + ((3,) + strip,) * 3,
        (k, s, p, q, packed, far, near, far_strip, near_strip),
        (field,) * 7 + (strip,),
    )
    sums = lax.all_to_all(mid[0], ("gx", "gy"), 0, 0, tiled=True)
    args = [pltpu.with_memory_space_constraint(x, pltpu.VMEM) for x in (sums, p) + tuple(mid[1:])]
    return pl.pallas_call(
        finish,
        name="finish",
        out_shape=(jax.ShapeDtypeStruct(own, F32),) * 2,
        in_specs=[VMEM] * len(args),
        out_specs=(ANY, ANY),
        scratch_shapes=[pltpu.VMEM(x, F32) for x in ((3,) + field, field, field, strip, strip, field, own, own)] + [pltpu.SemaphoreType.DMA((2,))],
    )(*args)


def local(permeability, saturation, pressure_old, source):
    outs = [one_sample(permeability[i], saturation[i], pressure_old[i], source) for i in range(permeability.shape[0])]
    return jnp.stack([o[0] for o in outs]), jnp.stack([o[1] for o in outs])


def solution(mesh):
    field = P(None, None, "gx", "gy")
    return jax.shard_map(local, mesh=mesh, in_specs=(field, field, field, P(None, "gx", "gy")), out_specs=(field, field), check_vma=False)
```

```python
import jax
import jax.numpy as jnp
from jax import lax
from jax.experimental import pallas as pl
from jax.experimental.pallas import tpu as pltpu
from jax.sharding import PartitionSpec as P


storage_term = 0.5
vertical_ratio = 0.1
step_ratio = 0.05
water_viscosity = 1.0
oil_viscosity = 2.0

NZ, ROWS, LANES, HALO = 16, 8, 128, 4
SPAN = 2 * ROWS
SEG = 16
TILES = NZ * SEG // LANES
PER = LANES // SEG
F32 = jnp.float32


def lanes(shape=(ROWS, LANES)):
    return lax.broadcasted_iota(jnp.int32, shape, len(shape) - 1)


def sublanes(shape=(ROWS, LANES)):
    return lax.broadcasted_iota(jnp.int32, shape, len(shape) - 2)


def turn(x, by, axis):
    n = x.shape[axis]
    if isinstance(by, int):
        by %= n
        if by == 0:
            return x
    return pltpu.roll(x, by, axis)


def total_mobility(s):
    return s * s / water_viscosity + (1.0 - s) * (1.0 - s) / oil_viscosity


def water_fraction(s):
    return s * s / water_viscosity / total_mobility(s)


def coefficient(ka, kb, ma, mb):
    return ka * kb * (ma + mb) / jnp.maximum(ka + kb, 1e-30)


def row_next(x):
    return turn(x, -1, 0)


def row_prev(x):
    return turn(x, 1, 0)


def col_next(x):
    return turn(x, -1, 1)


def col_prev(x):
    return turn(x, 1, 1)


def pack_columns(k_in, s_in, p_in, q_in, to_prev, to_next, k, s, p, q, sems):
    copies = [pltpu.make_async_copy(a, b, sems.at[i]) for i, (a, b) in enumerate(((k_in, k), (s_in, s), (p_in, p), (q_in, q)))]
    for c in copies:
        c.start()
    seg = lanes() % SEG // 4
    layer = lanes() // SEG
    first = [jnp.zeros((ROWS, LANES), F32) for _ in range(TILES)]
    last = [jnp.zeros((ROWS, LANES), F32) for _ in range(TILES)]
    for i, ref in enumerate((k, s, p, q)):
        copies[i].wait()
        for t in range(TILES):
            for zz in range(PER):
                x = ref[t * PER + zz]
                here = (layer == zz) & (seg == i)
                at = zz * SEG + 4 * i
                first[t] = jnp.where(here, turn(x, at, 1), first[t])
                last[t] = jnp.where(here, turn(x, at + HALO, 1), last[t])
    for t in range(TILES):
        to_prev[t] = first[t]
        to_next[t] = last[t]


def pair(at, a, b, to_far, to_near):
    odd = lax.axis_index("gx") % 2 == 1
    low = sublanes() < HALO
    before = jnp.where(low, a, turn(b, HALO, 0))
    after = jnp.where(low, turn(a, HALO, 0), b)
    to_far[at] = jnp.where(odd, after, before)
    to_near[at] = jnp.where(odd, before, after)


def pack_body(k, s, p, q, to_far, to_near):
    for z in range(NZ):
        pair(z, k[z], s[z], to_far, to_near)
        pair(NZ + z, p[z], q[z], to_far, to_near)


def pack_strip(own_first, own_last, from_prev, from_next, packed, to_far, to_near):
    seg = lanes() % SEG // 4
    for t in range(TILES):
        cols = []
        for i in range(4):
            x = turn(from_prev[t], -4 * i, 1)
            x = jnp.where(seg == 1, turn(own_first[t], 4 - 4 * i, 1), x)
            x = jnp.where(seg == 2, turn(own_last[t], 8 - 4 * i, 1), x)
            x = jnp.where(seg == 3, turn(from_next[t], 12 - 4 * i, 1), x)
            packed[i, t] = x
            cols.append(x)
        pair(t, cols[0], cols[1], to_far, to_near)
        pair(TILES + t, cols[2], cols[3], to_far, to_near)


def layer_next(x):
    edge = lanes((SPAN, LANES)) < LANES - SEG
    moved = [turn(t, -SEG, 1) for t in x]
    return [jnp.where(edge, moved[i], moved[(i + 1) % TILES]) for i in range(TILES)]


def layer_prev(x):
    edge = lanes((SPAN, LANES)) >= SEG
    moved = [turn(t, SEG, 1) for t in x]
    return [jnp.where(edge, moved[i], moved[(i - 1) % TILES]) for i in range(TILES)]


def each(f, *args):
    return [f(*a) for a in zip(*args)]


def packed_divergence(flows):
    fx, fy, fz = flows
    return each(lambda x, xp, y, yp, z, zp: (z - zp) + (x - xp) + (y - yp), fx, each(row_prev, fx), fy, each(col_prev, fy), fz, layer_prev(fz))


def packed_flows(terms, v):
    nexts = (each(row_next, v), each(col_next, v), layer_next(v))
    return [each(lambda c, a, b: c * (a - b), term, v, n) for term, n in zip(terms, nexts)]


def edge_next(y, packed_face, z):
    at = LANES - 1 - (z % PER * SEG + 11)
    return jnp.where(lanes((SPAN, LANES)) == LANES - 1, pltpu.roll(packed_face[z // PER], at, 1), y)


def edge_prev(y, packed_face, z):
    at = LANES - (z % PER * SEG + 3)
    return jnp.where(lanes((SPAN, LANES)) == 0, pltpu.roll(packed_face[z // PER], at, 1), col_prev(y))


def rows_inside():
    gx = lax.axis_index("gx")
    below = jnp.where(gx == lax.axis_size("gx") - 1, 0.0, 1.0)
    return jnp.where(sublanes() < HALO, below, jnp.where(gx == 0, 0.0, 1.0))


def cols_inside():
    gy = lax.axis_index("gy")
    after = jnp.where(gy == lax.axis_size("gy") - 1, 0.0, 1.0)
    seg = lanes() % SEG // 4
    return jnp.where(seg == 0, jnp.where(gy == 0, 0.0, 1.0), jnp.where(seg == 3, after, 1.0))


def halo_rows(at, far, near):
    odd = lax.axis_index("gx") % 2 == 1
    low = sublanes() < HALO
    below, above = jnp.where(odd, far[at], near[at]), jnp.where(odd, near[at], far[at])
    return jnp.where(low, below, turn(above, HALO, 0)), jnp.where(low, turn(below, HALO, 0), above)


def interior(k_own, s_own, p_own, q_own, far, near, s, q, f0, cx, cy, cz, diag, r, fpx, fpy, fpz, k, p, m):
    inside_rows = rows_inside()

    def assemble(z, _):
        ka, sa = halo_rows(z, far, near)
        pa, qa = halo_rows(NZ + z, far, near)
        k[z, :ROWS], k[z, ROWS:] = k_own[z], ka * inside_rows
        p[z, :ROWS], p[z, ROWS:] = p_own[z], pa
        q[z, :ROWS], q[z, ROWS:] = q_own[z], qa
        sat = jnp.concatenate([s_own[z], sa], 0)
        mobile = total_mobility(sat)
        s[z], m[z], f0[z] = sat, mobile, sat * sat / water_viscosity / mobile
        return _

    lax.fori_loop(0, NZ, assemble, 0, unroll=NZ // 2)
    last = lanes((SPAN, LANES)) == LANES - 1

    def first(z, carry):
        cz_prev, fz_prev = carry
        up = jnp.minimum(z + 1, NZ - 1)
        kz, pz, mz = k[z], p[z], m[z]
        ax = coefficient(kz, row_next(kz), mz, row_next(mz))
        ay = jnp.where(last, 0.0, coefficient(kz, col_next(kz), mz, col_next(mz)))
        az = jnp.where(z < NZ - 1, vertical_ratio, 0.0) * coefficient(kz, k[up], mz, m[up])
        fx = ax * (pz - row_next(pz))
        fy = ay * (pz - col_next(pz))
        fzz = az * (pz - p[up])
        diag[z] = storage_term + (az + cz_prev) + (ax + row_prev(ax)) + (ay + col_prev(ay))
        r[z] = q[z] - ((fzz - fz_prev) + (fx - row_prev(fx)) + (fy - col_prev(fy)))
        cx[z], cy[z], cz[z] = ax, ay, az
        fpx[z], fpy[z], fpz[z] = fx, fy, fzz
        return az, fzz

    zero = jnp.zeros((SPAN, LANES), F32)
    lax.fori_loop(0, NZ, first, (zero, zero), unroll=NZ // 2)


def middle(cx, cy_in, cz, diag, r_in, fpy_in, packed, far_strip, near_strip,
           sums, z0, v, fpy, fz, fv, s_pack, q_pack, fp_pack, fz_pack, fv_pack,
           cy, inv, r, cy_pack):
    inside_rows, inside_cols = rows_inside(), cols_inside()
    kp, sp, pp, qp = [], [], [], []
    for t in range(TILES):
        ka, sa = halo_rows(t, far_strip, near_strip)
        pa, qa = halo_rows(TILES + t, far_strip, near_strip)
        kp.append(jnp.concatenate([packed[0, t] * inside_cols, ka * inside_rows * inside_cols], 0))
        sp.append(jnp.concatenate([packed[1, t], sa], 0))
        pp.append(jnp.concatenate([packed[2, t], pa], 0))
        qp.append(jnp.concatenate([packed[3, t], qa], 0))
    mp = each(total_mobility, sp)
    tx = each(coefficient, kp, each(row_next, kp), mp, each(row_next, mp))
    ty = each(coefficient, kp, each(col_next, kp), mp, each(col_next, mp))
    tz = each(coefficient, kp, layer_next(kp), mp, layer_next(mp))
    tz = each(lambda c: vertical_ratio * c, tz)
    tz[-1] = jnp.where(lanes((SPAN, LANES)) < LANES - SEG, tz[-1], 0.0)
    terms = (tx, ty, tz)
    dsum = each(lambda x, xp, y, yp, z, zp: storage_term + (z + zp) + (x + xp) + (y + yp), tx, each(row_prev, tx), ty, each(col_prev, ty), tz, layer_prev(tz))
    ip = each(lambda d: 1.0 / d, dsum)
    flows_p = packed_flows(terms, pp)
    rp = each(lambda a, d: a - d, qp, packed_divergence(flows_p))
    zp0 = each(lambda a, b: a * b, rp, ip)
    flows_z = packed_flows(terms, zp0)
    gp = each(lambda a, d: storage_term * a + d, zp0, packed_divergence(flows_z))
    vp = each(lambda a, b, c: (a - b) * c, gp, rp, ip)
    flows_v = packed_flows(terms, vp)
    for t in range(TILES):
        s_pack[t], q_pack[t], cy_pack[t] = sp[t], qp[t], ty[t]
        for d in range(3):
            fp_pack[d, t], fz_pack[d, t], fv_pack[d, t] = flows_p[d][t], flows_z[d][t], flows_v[d][t]

    lane = lanes((SPAN, LANES))

    def ends(packed_face, z):
        at = z % PER * SEG
        face = packed_face[z // PER]
        return pltpu.roll(face, LANES - 1 - (at + 11), 1), pltpu.roll(face, LANES - (at + 3), 1)

    def first(z, _):
        after, before = ends(cy_pack, z)
        out, into = ends(fp_pack.at[1], z)
        last = lane == LANES - 1
        cy[z] = jnp.where(last, after, cy_in[z])
        fpy[z] = jnp.where(last, out, fpy_in[z])
        inverse = 1.0 / (diag[z] + jnp.where(last, after, jnp.where(lane == 0, before, 0.0)))
        res = r_in[z] - jnp.where(last, out, jnp.where(lane == 0, -into, 0.0))
        inv[z], r[z], z0[z] = inverse, res, res * inverse
        return _

    zero = jnp.zeros((SPAN, LANES), F32)
    zero8 = jnp.zeros((ROWS, LANES), F32)
    lax.fori_loop(0, NZ, first, 0, unroll=NZ)

    def second(z, carry):
        fz_prev, rz, zaz, rv, vaz = carry
        up = jnp.minimum(z + 1, NZ - 1)
        a = z0[z]
        fx = cx[z] * (a - row_next(a))
        fy = edge_next(cy[z] * (a - col_next(a)), fz_pack.at[1], z)
        fzz = cz[z] * (a - z0[up])
        g = storage_term * a + ((fzz - fz_prev) + (fx - row_prev(fx)) + (fy - edge_prev(fy, fz_pack.at[1], z)))
        fz[0, z], fz[1, z], fz[2, z] = fx, fy, fzz
        diff = g - r[z]
        b = diff * inv[z]
        v[z] = b
        a8, g8, d8, b8, r8 = a[:ROWS], g[:ROWS], diff[:ROWS], b[:ROWS], r[z, :ROWS]
        return fzz, rz + r8 * a8, zaz + a8 * g8, rv + a8 * d8, vaz + b8 * g8

    _, rz, zaz, rv, vaz = lax.fori_loop(0, NZ, second, (zero, zero8, zero8, zero8, zero8), unroll=NZ)

    def third(z, carry):
        fz_prev, vav = carry
        up = jnp.minimum(z + 1, NZ - 1)
        a = v[z]
        fx = cx[z] * (a - row_next(a))
        fy = edge_next(cy[z] * (a - col_next(a)), fv_pack.at[1], z)
        fzz = cz[z] * (a - v[up])
        fv[0, z], fv[1, z], fv[2, z] = fx, fy, fzz
        w = storage_term * a + ((fzz - fz_prev) + (fx - row_prev(fx)) + (fy - edge_prev(fy, fv_pack.at[1], z)))
        return fzz, vav + a[:ROWS] * w[:ROWS]

    _, vav = lax.fori_loop(0, NZ, third, (zero, zero8), unroll=NZ)
    row = zero8
    for i, x in enumerate((rz, zaz, rv, vaz, vav)):
        row = jnp.where(lanes() == i, jnp.sum(x), row)
    for i in range(sums.shape[0] // ROWS):
        sums[i * ROWS:(i + 1) * ROWS] = row


def finish(sums, p_own, z0, v, s, q, f0, fpx, fpy, fpz, fz, fv, s_pack, q_pack, fp_pack, fz_pack, fv_pack,
           pressure_out, s_out, flow, f1, s1, wy0_pack, wy1_pack, pressure, s_new, sems):
    total = jnp.sum(sums[...], axis=0, keepdims=True)
    lane = lanes((1, LANES))
    rz, zaz, rv, vaz, vav = (jnp.sum(jnp.where(lane == i, total, 0.0), axis=1, keepdims=True) for i in range(5))
    ratio = vaz / zaz
    bottom = vav - ratio * vaz
    top = rv - ratio * rz
    good = bottom > 0.0
    b = jnp.where(good, top / jnp.where(good, bottom, 1.0), 0.0)
    a = rz / zaz - b * ratio
    a16, b16 = (jnp.broadcast_to(x, (SPAN, LANES)) for x in (a, b))

    def gained(rate, fraction):
        return jnp.maximum(rate, 0.0) + jnp.minimum(rate, 0.0) * fraction

    def upwind(flux, here, there):
        return flux * jnp.where(flux > 0.0, here, there)

    flows = [[fp_pack[d, t] + a16 * fz_pack[d, t] + b16 * fv_pack[d, t] for t in range(TILES)] for d in range(3)]
    s_now = [s_pack[t] for t in range(TILES)]
    q_now = [q_pack[t] for t in range(TILES)]
    for step, keep in enumerate((wy0_pack, wy1_pack)):
        fr = each(water_fraction, s_now)
        nexts = (each(row_next, fr), each(col_next, fr), layer_next(fr))
        water = [each(upwind, fl, fr, n) for fl, n in zip(flows, nexts)]
        for t in range(TILES):
            keep[t] = water[1][t]
        if step == 0:
            s_now = each(lambda x, rate, f, d: x + step_ratio * (gained(rate, f) - d), s_now, q_now, fr, packed_divergence(water))

    def first(z, wz_prev):
        up = jnp.minimum(z + 1, NZ - 1)
        fx, fy, fzz = (fp[z] + a16 * fz[d, z] + b16 * fv[d, z] for d, fp in enumerate((fpx, fpy, fpz)))
        flow[0, z], flow[1, z], flow[2, z] = fx, fy, fzz
        pressure[z] = p_own[z] + a16[:ROWS] * z0[z, :ROWS] + b16[:ROWS] * v[z, :ROWS]
        f = f0[z]
        wx = upwind(fx, f, row_next(f))
        wy = edge_next(upwind(fy, f, col_next(f)), wy0_pack, z)
        wz = upwind(fzz, f, f0[up])
        new = s[z] + step_ratio * (gained(q[z], f) - ((wz - wz_prev) + (wx - row_prev(wx)) + (wy - edge_prev(wy, wy0_pack, z))))
        s1[z] = new
        f1[z] = water_fraction(new)
        return wz

    lax.fori_loop(0, NZ, first, jnp.zeros((SPAN, LANES), F32), unroll=NZ)
    send = pltpu.make_async_copy(pressure, pressure_out, sems.at[0])
    send.start()

    def second(z, wz_prev):
        up = jnp.minimum(z + 1, NZ - 1)
        f = f1[z]
        wx = upwind(flow[0, z], f, row_next(f))
        wy = edge_next(upwind(flow[1, z], f, col_next(f)), wy1_pack, z)
        wz = upwind(flow[2, z, :ROWS], f[:ROWS], f1[up, :ROWS])
        east = (wy - edge_prev(wy, wy1_pack, z))[:ROWS]
        s_new[z] = s1[z, :ROWS] + step_ratio * (gained(q[z, :ROWS], f[:ROWS]) - ((wz - wz_prev) + (wx - row_prev(wx))[:ROWS] + east))
        return wz

    lax.fori_loop(0, NZ, second, jnp.zeros((ROWS, LANES), F32), unroll=NZ)
    send_s = pltpu.make_async_copy(s_new, s_out, sems.at[1])
    send_s.start()
    send.wait()
    send_s.wait()


VMEM = pl.BlockSpec(memory_space=pltpu.VMEM)
ANY = pl.BlockSpec(memory_space=pl.ANY)
SCRATCH = pltpu.CompilerParams(vmem_limit_bytes=8 << 20)


def call(body, outs, args, scratch=()):
    args = [pltpu.with_memory_space_constraint(x, pltpu.VMEM) for x in args]
    return pl.pallas_call(
        body,
        compiler_params=SCRATCH,
        out_shape=tuple(pltpu.VMEM(s, F32) for s in outs),
        in_specs=[VMEM] * len(args),
        out_specs=tuple(VMEM for _ in outs),
        scratch_shapes=[pltpu.VMEM(s, F32) for s in scratch],
    )(*args)


def ring(x, axis, by):
    n = lax.axis_size(axis)
    return lax.ppermute(x, axis, [(i, (i + by) % n) for i in range(n)])


def trade(x, first):
    nx, ny = lax.axis_size("gx"), lax.axis_size("gy")
    other = {}
    for i in range(first, nx - 1, 2):
        other[i], other[i + 1] = i + 1, i
    pairs = [(i * ny + j, other[i] * ny + j if i in other else i * ny + (j ^ 1)) for i in range(nx) for j in range(ny)]
    return lax.ppermute(x, ("gx", "gy"), pairs)


def one_sample(k, s, p, q):
    own = (NZ, ROWS, LANES)
    assert k.shape == own
    cols = (TILES, ROWS, LANES)
    first, last, k, s, p, q = pl.pallas_call(
        pack_columns,
        name="pack_columns",
        compiler_params=SCRATCH,
        out_shape=tuple(pltpu.VMEM(x, F32) for x in (cols, cols, own, own, own, own)),
        in_specs=[ANY] * 4,
        out_specs=(VMEM,) * 6,
        scratch_shapes=[pltpu.SemaphoreType.DMA((4,))],
    )(*(pltpu.with_memory_space_constraint(x, pltpu.HBM) for x in (k, s, p, q)))
    from_prev = ring(last, "gy", 1)
    from_next = ring(first, "gy", -1)
    body, strips = (2 * NZ, ROWS, LANES), (2 * TILES, ROWS, LANES)
    to_far, to_near = call(pack_body, (body, body), (k, s, p, q))
    far = trade(to_far, 1)
    near = trade(to_near, 0)
    packed, to_far, to_near = call(pack_strip, ((4,) + cols, strips, strips), (first, last, from_prev, from_next))
    far_strip = trade(to_far, 1)
    near_strip = trade(to_near, 0)
    field, strip = (NZ, SPAN, LANES), (TILES, SPAN, LANES)
    s, q, f0, cx, cy, cz, diag, r, fpx, fpy, fpz = call(interior, (field,) * 11, (k, s, p, q, far, near), (field,) * 3)
    size = lax.axis_size("gx") * lax.axis_size("gy")
    sums, z0, v, fpy, *rest = call(
        middle,
        ((size, LANES),) + (field,) * 3 + ((3,) + field,) * 2 + (strip,) * 2 + ((3,) + strip,) * 3,
        (cx, cy, cz, diag, r, fpy, packed, far_strip, near_strip),
        (field,) * 3 + (strip,),
    )
    sums = lax.all_to_all(sums, ("gx", "gy"), 0, 0, tiled=True)
    args = [pltpu.with_memory_space_constraint(x, pltpu.VMEM) for x in (sums, p, z0, v, s, q, f0, fpx, fpy, fpz, *rest)]
    return pl.pallas_call(
        finish,
        name="finish",
        compiler_params=SCRATCH,
        out_shape=(jax.ShapeDtypeStruct(own, F32),) * 2,
        in_specs=[VMEM] * len(args),
        out_specs=(ANY, ANY),
        scratch_shapes=[pltpu.VMEM(x, F32) for x in ((3,) + field, field, field, strip, strip, own, own)] + [pltpu.SemaphoreType.DMA((2,))],
    )(*args)


def local(permeability, saturation, pressure_old, source):
    outs = [one_sample(permeability[i], saturation[i], pressure_old[i], source) for i in range(permeability.shape[0])]
    return jnp.stack([o[0] for o in outs]), jnp.stack([o[1] for o in outs])


def solution(mesh):
    field = P(None, None, "gx", "gy")
    return jax.shard_map(local, mesh=mesh, in_specs=(field, field, field, P(None, "gx", "gy")), out_specs=(field, field), check_vma=False)
```

```python
import jax
import jax.numpy as jnp
from jax import lax
from jax.experimental import pallas as pl
from jax.experimental.pallas import tpu as pltpu
from jax.sharding import PartitionSpec as P


storage_term = 0.5
vertical_ratio = 0.1
step_ratio = 0.05
water_viscosity = 1.0
oil_viscosity = 2.0

NZ, ROWS, LANES, HALO = 16, 8, 128, 4
SPAN = 2 * ROWS
SEG = 16
TILES = NZ * SEG // LANES
PER = LANES // SEG
F32 = jnp.float32


def lanes(shape=(ROWS, LANES)):
    return lax.broadcasted_iota(jnp.int32, shape, len(shape) - 1)


def sublanes(shape=(ROWS, LANES)):
    return lax.broadcasted_iota(jnp.int32, shape, len(shape) - 2)


def turn(x, by, axis):
    n = x.shape[axis]
    if isinstance(by, int):
        by %= n
        if by == 0:
            return x
    return pltpu.roll(x, by, axis)


def total_mobility(s):
    return s * s / water_viscosity + (1.0 - s) * (1.0 - s) / oil_viscosity


def water_fraction(s):
    return s * s / water_viscosity / total_mobility(s)


def coefficient(ka, kb, ma, mb):
    return ka * kb * (ma + mb) / jnp.maximum(ka + kb, 1e-30)


def row_next(x):
    return turn(x, -1, 0)


def row_prev(x):
    return turn(x, 1, 0)


def col_next(x):
    return turn(x, -1, 1)


def col_prev(x):
    return turn(x, 1, 1)


def pack_columns(k_in, s_in, p_in, q_in, to_prev, to_next, k, s, p, q, sems):
    copies = [pltpu.make_async_copy(a, b, sems.at[i]) for i, (a, b) in enumerate(((k_in, k), (s_in, s), (p_in, p), (q_in, q)))]
    for c in copies:
        c.start()
    quad = lanes() // 4
    quads = LANES // 4
    first = [jnp.zeros((ROWS, LANES), F32) for _ in range(TILES)]
    last = [jnp.zeros((ROWS, LANES), F32) for _ in range(TILES)]
    for i, ref in enumerate((k, s, p, q)):
        copies[i].wait()
        for t in range(TILES):
            for zz in range(PER):
                x = ref[t * PER + zz]
                at = zz * 4 + i
                x = turn(x, 4 * at + HALO, 1)
                last[t] = jnp.where(quad == at, x, last[t])
                first[t] = jnp.where(quad == (at + 1) % quads, x, first[t])
    for t in range(TILES):
        to_prev[t] = turn(first[t], -HALO, 1)
        to_next[t] = last[t]


def pair(at, a, b, to_far, to_near):
    odd = lax.axis_index("gx") % 2 == 1
    low = sublanes() < HALO
    before = jnp.where(low, a, turn(b, HALO, 0))
    after = jnp.where(low, turn(a, HALO, 0), b)
    to_far[at] = jnp.where(odd, after, before)
    to_near[at] = jnp.where(odd, before, after)


def pack_body(k, s, p, q, to_far, to_near):
    for z in range(NZ):
        pair(z, k[z], s[z], to_far, to_near)
        pair(NZ + z, p[z], q[z], to_far, to_near)


def pack_strip(own_first, own_last, from_prev, from_next, packed, to_far, to_near):
    seg = lanes() % SEG // 4
    for t in range(TILES):
        cols = []
        for i in range(4):
            x = turn(from_prev[t], -4 * i, 1)
            x = jnp.where(seg == 1, turn(own_first[t], 4 - 4 * i, 1), x)
            x = jnp.where(seg == 2, turn(own_last[t], 8 - 4 * i, 1), x)
            x = jnp.where(seg == 3, turn(from_next[t], 12 - 4 * i, 1), x)
            packed[i, t] = x
            cols.append(x)
        pair(t, cols[0], cols[1], to_far, to_near)
        pair(TILES + t, cols[2], cols[3], to_far, to_near)


def layer_next(x):
    edge = lanes((SPAN, LANES)) < LANES - SEG
    moved = [turn(t, -SEG, 1) for t in x]
    return [jnp.where(edge, moved[i], moved[(i + 1) % TILES]) for i in range(TILES)]


def layer_prev(x):
    edge = lanes((SPAN, LANES)) >= SEG
    moved = [turn(t, SEG, 1) for t in x]
    return [jnp.where(edge, moved[i], moved[(i - 1) % TILES]) for i in range(TILES)]


def each(f, *args):
    return [f(*a) for a in zip(*args)]


def packed_divergence(flows):
    fx, fy, fz = flows
    return each(lambda x, xp, y, yp, z, zp: (z - zp) + (x - xp) + (y - yp), fx, each(row_prev, fx), fy, each(col_prev, fy), fz, layer_prev(fz))


def packed_flows(terms, v):
    nexts = (each(row_next, v), each(col_next, v), layer_next(v))
    return [each(lambda c, a, b: c * (a - b), term, v, n) for term, n in zip(terms, nexts)]


def join_ends(face):
    behind = lanes((SPAN, LANES)) % SEG == 11
    return jnp.where(behind, face, turn(face, 9, 1))


def ends(joined, z):
    return pltpu.roll(joined[z // PER], LANES - 1 - (z % PER * SEG + 11), 1)


def edge_next(y, end):
    return jnp.where(lanes((SPAN, LANES)) == LANES - 1, end, y)


def edge_prev(y, end):
    return jnp.where(lanes((SPAN, LANES)) == 0, end, col_prev(y))


def rows_inside():
    gx = lax.axis_index("gx")
    below = jnp.where(gx == lax.axis_size("gx") - 1, 0.0, 1.0)
    return jnp.where(sublanes() < HALO, below, jnp.where(gx == 0, 0.0, 1.0))


def cols_inside():
    gy = lax.axis_index("gy")
    after = jnp.where(gy == lax.axis_size("gy") - 1, 0.0, 1.0)
    seg = lanes() % SEG // 4
    return jnp.where(seg == 0, jnp.where(gy == 0, 0.0, 1.0), jnp.where(seg == 3, after, 1.0))


def halo_rows(at, far, near):
    odd = lax.axis_index("gx") % 2 == 1
    low = sublanes() < HALO
    below, above = jnp.where(odd, far[at], near[at]), jnp.where(odd, near[at], far[at])
    return jnp.where(low, below, turn(above, HALO, 0)), jnp.where(low, turn(below, HALO, 0), above)


def interior(k_own, s_own, p_own, q_own, far, near, s, q, f0, cx, cy, cz, diag, r, fpx, fpy, fpz, k, p, m):
    inside_rows = rows_inside()

    def assemble(z, _):
        ka, sa = halo_rows(z, far, near)
        pa, qa = halo_rows(NZ + z, far, near)
        k[z, :ROWS], k[z, ROWS:] = k_own[z], ka * inside_rows
        p[z, :ROWS], p[z, ROWS:] = p_own[z], pa
        q[z, :ROWS], q[z, ROWS:] = q_own[z], qa
        sat = jnp.concatenate([s_own[z], sa], 0)
        mobile = total_mobility(sat)
        s[z], m[z], f0[z] = sat, mobile, sat * sat / water_viscosity / mobile
        return _

    lax.fori_loop(0, NZ, assemble, 0, unroll=NZ // 2)
    last = lanes((SPAN, LANES)) == LANES - 1

    def first(z, carry):
        cz_prev, fz_prev = carry
        up = jnp.minimum(z + 1, NZ - 1)
        kz, pz, mz = k[z], p[z], m[z]
        ax = coefficient(kz, row_next(kz), mz, row_next(mz))
        ay = jnp.where(last, 0.0, coefficient(kz, col_next(kz), mz, col_next(mz)))
        az = jnp.where(z < NZ - 1, vertical_ratio, 0.0) * coefficient(kz, k[up], mz, m[up])
        fx = ax * (pz - row_next(pz))
        fy = ay * (pz - col_next(pz))
        fzz = az * (pz - p[up])
        diag[z] = storage_term + (az + cz_prev) + (ax + row_prev(ax)) + (ay + col_prev(ay))
        r[z] = q[z] - ((fzz - fz_prev) + (fx - row_prev(fx)) + (fy - col_prev(fy)))
        cx[z], cy[z], cz[z] = ax, ay, az
        fpx[z], fpy[z], fpz[z] = fx, fy, fzz
        return az, fzz

    zero = jnp.zeros((SPAN, LANES), F32)
    lax.fori_loop(0, NZ, first, (zero, zero), unroll=NZ // 2)


def middle(cx, cy_in, cz, diag, r_in, fpy_in, packed, far_strip, near_strip,
           sums, z0, v, fpy, fz, fv, s_pack, q_pack, fp_pack, fz_pack, fv_pack,
           cy, inv, r, cy_ends, fp_ends, fz_ends, fv_ends):
    inside_rows, inside_cols = rows_inside(), cols_inside()
    kp, sp, pp, qp = [], [], [], []
    for t in range(TILES):
        ka, sa = halo_rows(t, far_strip, near_strip)
        pa, qa = halo_rows(TILES + t, far_strip, near_strip)
        kp.append(jnp.concatenate([packed[0, t] * inside_cols, ka * inside_rows * inside_cols], 0))
        sp.append(jnp.concatenate([packed[1, t], sa], 0))
        pp.append(jnp.concatenate([packed[2, t], pa], 0))
        qp.append(jnp.concatenate([packed[3, t], qa], 0))
    mp = each(total_mobility, sp)
    tx = each(coefficient, kp, each(row_next, kp), mp, each(row_next, mp))
    ty = each(coefficient, kp, each(col_next, kp), mp, each(col_next, mp))
    tz = each(coefficient, kp, layer_next(kp), mp, layer_next(mp))
    tz = each(lambda c: vertical_ratio * c, tz)
    tz[-1] = jnp.where(lanes((SPAN, LANES)) < LANES - SEG, tz[-1], 0.0)
    terms = (tx, ty, tz)
    dsum = each(lambda x, xp, y, yp, z, zp: storage_term + (z + zp) + (x + xp) + (y + yp), tx, each(row_prev, tx), ty, each(col_prev, ty), tz, layer_prev(tz))
    ip = each(lambda d: 1.0 / d, dsum)
    flows_p = packed_flows(terms, pp)
    rp = each(lambda a, d: a - d, qp, packed_divergence(flows_p))
    zp0 = each(lambda a, b: a * b, rp, ip)
    flows_z = packed_flows(terms, zp0)
    gp = each(lambda a, d: storage_term * a + d, zp0, packed_divergence(flows_z))
    vp = each(lambda a, b, c: (a - b) * c, gp, rp, ip)
    flows_v = packed_flows(terms, vp)
    for t in range(TILES):
        s_pack[t], q_pack[t] = sp[t], qp[t]
        for joined, face in ((cy_ends, ty), (fp_ends, flows_p[1]), (fz_ends, flows_z[1]), (fv_ends, flows_v[1])):
            joined[t] = join_ends(face[t])
        for d in range(3):
            fp_pack[d, t], fz_pack[d, t], fv_pack[d, t] = flows_p[d][t], flows_z[d][t], flows_v[d][t]

    lane = lanes((SPAN, LANES))

    def first(z, _):
        c, f = ends(cy_ends, z), ends(fp_ends, z)
        last = lane == LANES - 1
        cy[z] = jnp.where(last, c, cy_in[z])
        fpy[z] = jnp.where(last, f, fpy_in[z])
        inverse = 1.0 / (diag[z] + jnp.where(last | (lane == 0), c, 0.0))
        res = r_in[z] - jnp.where(last, f, jnp.where(lane == 0, -f, 0.0))
        inv[z], r[z], z0[z] = inverse, res, res * inverse
        return _

    zero = jnp.zeros((SPAN, LANES), F32)
    zero8 = jnp.zeros((ROWS, LANES), F32)
    lax.fori_loop(0, NZ, first, 0, unroll=NZ)

    def second(z, carry):
        fz_prev, rz, zaz, rv, vaz = carry
        up = jnp.minimum(z + 1, NZ - 1)
        a = z0[z]
        fx = cx[z] * (a - row_next(a))
        end = ends(fz_ends, z)
        fy = edge_next(cy[z] * (a - col_next(a)), end)
        fzz = cz[z] * (a - z0[up])
        g = storage_term * a + ((fzz - fz_prev) + (fx - row_prev(fx)) + (fy - edge_prev(fy, end)))
        fz[0, z], fz[1, z], fz[2, z] = fx, fy, fzz
        diff = g - r[z]
        b = diff * inv[z]
        v[z] = b
        a8, g8, d8, b8, r8 = a[:ROWS], g[:ROWS], diff[:ROWS], b[:ROWS], r[z, :ROWS]
        return fzz, rz + r8 * a8, zaz + a8 * g8, rv + a8 * d8, vaz + b8 * g8

    _, rz, zaz, rv, vaz = lax.fori_loop(0, NZ, second, (zero, zero8, zero8, zero8, zero8), unroll=NZ)

    def third(z, carry):
        fz_prev, vav = carry
        up = jnp.minimum(z + 1, NZ - 1)
        a = v[z]
        fx = cx[z] * (a - row_next(a))
        end = ends(fv_ends, z)
        fy = edge_next(cy[z] * (a - col_next(a)), end)
        fzz = cz[z] * (a - v[up])
        fv[0, z], fv[1, z], fv[2, z] = fx, fy, fzz
        w = storage_term * a + ((fzz - fz_prev) + (fx - row_prev(fx)) + (fy - edge_prev(fy, end)))
        return fzz, vav + a[:ROWS] * w[:ROWS]

    _, vav = lax.fori_loop(0, NZ, third, (zero, zero8), unroll=NZ)
    row = zero8
    for i, x in enumerate((rz, zaz, rv, vaz, vav)):
        row = jnp.where(lanes() == i, jnp.sum(x), row)
    for i in range(sums.shape[0] // ROWS):
        sums[i * ROWS:(i + 1) * ROWS] = row


def finish(sums, p_own, z0, v, s, q, f0, fpx, fpy, fpz, fz, fv, s_pack, q_pack, fp_pack, fz_pack, fv_pack,
           pressure_out, s_out, flow, f1, s1, wy0_ends, wy1_ends, pressure, s_new, sems):
    total = jnp.sum(sums[...], axis=0, keepdims=True)
    lane = lanes((1, LANES))
    rz, zaz, rv, vaz, vav = (jnp.sum(jnp.where(lane == i, total, 0.0), axis=1, keepdims=True) for i in range(5))
    ratio = vaz / zaz
    bottom = vav - ratio * vaz
    top = rv - ratio * rz
    good = bottom > 0.0
    b = jnp.where(good, top / jnp.where(good, bottom, 1.0), 0.0)
    a = rz / zaz - b * ratio
    a16, b16 = (jnp.broadcast_to(x, (SPAN, LANES)) for x in (a, b))

    def gained(rate, fraction):
        return jnp.maximum(rate, 0.0) + jnp.minimum(rate, 0.0) * fraction

    def upwind(flux, here, there):
        return flux * jnp.where(flux > 0.0, here, there)

    flows = [[fp_pack[d, t] + a16 * fz_pack[d, t] + b16 * fv_pack[d, t] for t in range(TILES)] for d in range(3)]
    s_now = [s_pack[t] for t in range(TILES)]
    q_now = [q_pack[t] for t in range(TILES)]
    for step, keep in enumerate((wy0_ends, wy1_ends)):
        fr = each(water_fraction, s_now)
        nexts = (each(row_next, fr), each(col_next, fr), layer_next(fr))
        water = [each(upwind, fl, fr, n) for fl, n in zip(flows, nexts)]
        for t in range(TILES):
            keep[t] = join_ends(water[1][t])
        if step == 0:
            s_now = each(lambda x, rate, f, d: x + step_ratio * (gained(rate, f) - d), s_now, q_now, fr, packed_divergence(water))

    def first(z, wz_prev):
        up = jnp.minimum(z + 1, NZ - 1)
        fx, fy, fzz = (fp[z] + a16 * fz[d, z] + b16 * fv[d, z] for d, fp in enumerate((fpx, fpy, fpz)))
        flow[0, z], flow[1, z], flow[2, z] = fx, fy, fzz
        pressure[z] = p_own[z] + a16[:ROWS] * z0[z, :ROWS] + b16[:ROWS] * v[z, :ROWS]
        f = f0[z]
        wx = upwind(fx, f, row_next(f))
        end = ends(wy0_ends, z)
        wy = edge_next(upwind(fy, f, col_next(f)), end)
        wz = upwind(fzz, f, f0[up])
        new = s[z] + step_ratio * (gained(q[z], f) - ((wz - wz_prev) + (wx - row_prev(wx)) + (wy - edge_prev(wy, end))))
        s1[z] = new
        f1[z] = water_fraction(new)
        return wz

    lax.fori_loop(0, NZ, first, jnp.zeros((SPAN, LANES), F32), unroll=NZ)
    send = pltpu.make_async_copy(pressure, pressure_out, sems.at[0])
    send.start()

    def second(z, wz_prev):
        up = jnp.minimum(z + 1, NZ - 1)
        f = f1[z]
        wx = upwind(flow[0, z], f, row_next(f))
        end = ends(wy1_ends, z)
        wy = edge_next(upwind(flow[1, z], f, col_next(f)), end)
        wz = upwind(flow[2, z, :ROWS], f[:ROWS], f1[up, :ROWS])
        east = (wy - edge_prev(wy, end))[:ROWS]
        s_new[z] = s1[z, :ROWS] + step_ratio * (gained(q[z, :ROWS], f[:ROWS]) - ((wz - wz_prev) + (wx - row_prev(wx))[:ROWS] + east))
        return wz

    lax.fori_loop(0, NZ, second, jnp.zeros((ROWS, LANES), F32), unroll=NZ)
    send_s = pltpu.make_async_copy(s_new, s_out, sems.at[1])
    send_s.start()
    send.wait()
    send_s.wait()


VMEM = pl.BlockSpec(memory_space=pltpu.VMEM)
ANY = pl.BlockSpec(memory_space=pl.ANY)
SCRATCH = pltpu.CompilerParams(vmem_limit_bytes=8 << 20)


def call(body, outs, args, scratch=()):
    args = [pltpu.with_memory_space_constraint(x, pltpu.VMEM) for x in args]
    return pl.pallas_call(
        body,
        compiler_params=SCRATCH,
        out_shape=tuple(pltpu.VMEM(s, F32) for s in outs),
        in_specs=[VMEM] * len(args),
        out_specs=tuple(VMEM for _ in outs),
        scratch_shapes=[pltpu.VMEM(s, F32) for s in scratch],
    )(*args)


def ring(x, axis, by):
    n = lax.axis_size(axis)
    return lax.ppermute(x, axis, [(i, (i + by) % n) for i in range(n)])


def trade(x, first):
    nx, ny = lax.axis_size("gx"), lax.axis_size("gy")
    other = {}
    for i in range(first, nx - 1, 2):
        other[i], other[i + 1] = i + 1, i
    pairs = [(i * ny + j, other[i] * ny + j if i in other else i * ny + (j ^ 1)) for i in range(nx) for j in range(ny)]
    return lax.ppermute(x, ("gx", "gy"), pairs)


def one_sample(k, s, p, q):
    own = (NZ, ROWS, LANES)
    assert k.shape == own
    cols = (TILES, ROWS, LANES)
    first, last, k, s, p, q = pl.pallas_call(
        pack_columns,
        name="pack_columns",
        compiler_params=SCRATCH,
        out_shape=tuple(pltpu.VMEM(x, F32) for x in (cols, cols, own, own, own, own)),
        in_specs=[ANY] * 4,
        out_specs=(VMEM,) * 6,
        scratch_shapes=[pltpu.SemaphoreType.DMA((4,))],
    )(*(pltpu.with_memory_space_constraint(x, pltpu.HBM) for x in (k, s, p, q)))
    from_prev = ring(last, "gy", 1)
    from_next = ring(first, "gy", -1)
    body, strips = (2 * NZ, ROWS, LANES), (2 * TILES, ROWS, LANES)
    to_far, to_near = call(pack_body, (body, body), (k, s, p, q))
    far = trade(to_far, 1)
    near = trade(to_near, 0)
    packed, to_far, to_near = call(pack_strip, ((4,) + cols, strips, strips), (first, last, from_prev, from_next))
    far_strip = trade(to_far, 1)
    near_strip = trade(to_near, 0)
    field, strip = (NZ, SPAN, LANES), (TILES, SPAN, LANES)
    s, q, f0, cx, cy, cz, diag, r, fpx, fpy, fpz = call(interior, (field,) * 11, (k, s, p, q, far, near), (field,) * 3)
    size = lax.axis_size("gx") * lax.axis_size("gy")
    sums, z0, v, fpy, *rest = call(
        middle,
        ((size, LANES),) + (field,) * 3 + ((3,) + field,) * 2 + (strip,) * 2 + ((3,) + strip,) * 3,
        (cx, cy, cz, diag, r, fpy, packed, far_strip, near_strip),
        (field,) * 3 + (strip,) * 4,
    )
    sums = lax.all_to_all(sums, ("gx", "gy"), 0, 0, tiled=True)
    args = [pltpu.with_memory_space_constraint(x, pltpu.VMEM) for x in (sums, p, z0, v, s, q, f0, fpx, fpy, fpz, *rest)]
    return pl.pallas_call(
        finish,
        name="finish",
        compiler_params=SCRATCH,
        out_shape=(jax.ShapeDtypeStruct(own, F32),) * 2,
        in_specs=[VMEM] * len(args),
        out_specs=(ANY, ANY),
        scratch_shapes=[pltpu.VMEM(x, F32) for x in ((3,) + field, field, field, strip, strip, own, own)] + [pltpu.SemaphoreType.DMA((2,))],
    )(*args)


def local(permeability, saturation, pressure_old, source):
    outs = [one_sample(permeability[i], saturation[i], pressure_old[i], source) for i in range(permeability.shape[0])]
    return jnp.stack([o[0] for o in outs]), jnp.stack([o[1] for o in outs])


def solution(mesh):
    field = P(None, None, "gx", "gy")
    return jax.shard_map(local, mesh=mesh, in_specs=(field, field, field, P(None, "gx", "gy")), out_specs=(field, field), check_vma=False)
```

```python
import jax
import jax.numpy as jnp
from jax import lax
from jax.experimental import pallas as pl
from jax.experimental.pallas import tpu as pltpu
from jax.sharding import PartitionSpec as P


storage_term = 0.5
vertical_ratio = 0.1
step_ratio = 0.05
water_viscosity = 1.0
oil_viscosity = 2.0

NZ, ROWS, LANES, HALO = 16, 8, 128, 4
SPAN = 2 * ROWS
SEG = 16
TILES = NZ * SEG // LANES
PER = LANES // SEG
F32 = jnp.float32
PIECE = 8


def lanes(shape=(ROWS, LANES)):
    return lax.broadcasted_iota(jnp.int32, shape, len(shape) - 1)


def sublanes(shape=(ROWS, LANES)):
    return lax.broadcasted_iota(jnp.int32, shape, len(shape) - 2)


def turn(x, by, axis):
    n = x.shape[axis]
    if isinstance(by, int):
        by %= n
        if by == 0:
            return x
    return pltpu.roll(x, by, axis)


def total_mobility(s):
    return s * s / water_viscosity + (1.0 - s) * (1.0 - s) / oil_viscosity


def water_fraction(s):
    return s * s / water_viscosity / total_mobility(s)


def coefficient(ka, kb, ma, mb):
    return ka * kb * (ma + mb) / jnp.maximum(ka + kb, 1e-30)


def row_next(x):
    return turn(x, -1, 0)


def row_prev(x):
    return turn(x, 1, 0)


def col_next(x):
    return turn(x, -1, 1)


def col_prev(x):
    return turn(x, 1, 1)


def pack_columns(k_in, s_in, p_in, q_in, to_prev, to_next, k, s, p, q, sems):
    pieces = range(0, NZ, PIECE)
    copies = [
        [pltpu.make_async_copy(a.at[z:z + PIECE], b.at[z:z + PIECE], sems.at[i, z // PIECE]) for i, (a, b) in enumerate(((k_in, k), (s_in, s), (p_in, p), (q_in, q)))]
        for z in pieces
    ]
    for piece in copies:
        for c in piece:
            c.start()
    quad = lanes() // 4
    quads = LANES // 4
    first = [jnp.zeros((ROWS, LANES), F32) for _ in range(TILES)]
    last = [jnp.zeros((ROWS, LANES), F32) for _ in range(TILES)]
    for z in range(NZ):
        if z % PIECE == 0:
            for c in copies[z // PIECE]:
                c.wait()
        t, zz = divmod(z, PER)
        for i, ref in enumerate((k, s, p, q)):
            at = zz * 4 + i
            x = turn(ref[z], 4 * at + HALO, 1)
            last[t] = jnp.where(quad == at, x, last[t])
            first[t] = jnp.where(quad == (at + 1) % quads, x, first[t])
    for t in range(TILES):
        to_prev[t] = turn(first[t], -HALO, 1)
        to_next[t] = last[t]


def pair(at, a, b, to_far, to_near):
    odd = lax.axis_index("gx") % 2 == 1
    low = sublanes() < HALO
    before = jnp.where(low, a, turn(b, HALO, 0))
    after = jnp.where(low, turn(a, HALO, 0), b)
    to_far[at] = jnp.where(odd, after, before)
    to_near[at] = jnp.where(odd, before, after)


def pack_body(k, s, p, q, to_far, to_near):
    for z in range(NZ):
        pair(z, k[z], s[z], to_far, to_near)
        pair(NZ + z, p[z], q[z], to_far, to_near)


def pack_strip(own_first, own_last, from_prev, from_next, packed, to_far, to_near):
    seg = lanes() % SEG // 4
    for t in range(TILES):
        cols = []
        for i in range(4):
            x = turn(from_prev[t], -4 * i, 1)
            x = jnp.where(seg == 1, turn(own_first[t], 4 - 4 * i, 1), x)
            x = jnp.where(seg == 2, turn(own_last[t], 8 - 4 * i, 1), x)
            x = jnp.where(seg == 3, turn(from_next[t], 12 - 4 * i, 1), x)
            packed[i, t] = x
            cols.append(x)
        pair(t, cols[0], cols[1], to_far, to_near)
        pair(TILES + t, cols[2], cols[3], to_far, to_near)


def layer_next(x):
    edge = lanes((SPAN, LANES)) < LANES - SEG
    moved = [turn(t, -SEG, 1) for t in x]
    return [jnp.where(edge, moved[i], moved[(i + 1) % TILES]) for i in range(TILES)]


def layer_prev(x):
    edge = lanes((SPAN, LANES)) >= SEG
    moved = [turn(t, SEG, 1) for t in x]
    return [jnp.where(edge, moved[i], moved[(i - 1) % TILES]) for i in range(TILES)]


def each(f, *args):
    return [f(*a) for a in zip(*args)]


def packed_divergence(flows):
    fx, fy, fz = flows
    return each(lambda x, xp, y, yp, z, zp: (z - zp) + (x - xp) + (y - yp), fx, each(row_prev, fx), fy, each(col_prev, fy), fz, layer_prev(fz))


def packed_flows(terms, v):
    nexts = (each(row_next, v), each(col_next, v), layer_next(v))
    return [each(lambda c, a, b: c * (a - b), term, v, n) for term, n in zip(terms, nexts)]


def join_ends(face):
    behind = lanes((SPAN, LANES)) % SEG == 11
    return jnp.where(behind, face, turn(face, 9, 1))


def ends(joined, z):
    return pltpu.roll(joined[z // PER], LANES - 1 - (z % PER * SEG + 11), 1)


def edge_next(y, end):
    return jnp.where(lanes((SPAN, LANES)) == LANES - 1, end, y)


def edge_prev(y, end):
    return jnp.where(lanes((SPAN, LANES)) == 0, end, col_prev(y))


def rows_inside():
    gx = lax.axis_index("gx")
    below = jnp.where(gx == lax.axis_size("gx") - 1, 0.0, 1.0)
    return jnp.where(sublanes() < HALO, below, jnp.where(gx == 0, 0.0, 1.0))


def cols_inside():
    gy = lax.axis_index("gy")
    after = jnp.where(gy == lax.axis_size("gy") - 1, 0.0, 1.0)
    seg = lanes() % SEG // 4
    return jnp.where(seg == 0, jnp.where(gy == 0, 0.0, 1.0), jnp.where(seg == 3, after, 1.0))


def halo_rows(at, far, near):
    odd = lax.axis_index("gx") % 2 == 1
    low = sublanes() < HALO
    below, above = jnp.where(odd, far[at], near[at]), jnp.where(odd, near[at], far[at])
    return jnp.where(low, below, turn(above, HALO, 0)), jnp.where(low, turn(below, HALO, 0), above)


def interior(k_own, s_own, p_own, q_own, far, near, s, q, f0, cx, cy, cz, diag, r, fpx, fpy, fpz, k, p, m):
    inside_rows = rows_inside()

    def assemble(z, _):
        ka, sa = halo_rows(z, far, near)
        pa, qa = halo_rows(NZ + z, far, near)
        k[z, :ROWS], k[z, ROWS:] = k_own[z], ka * inside_rows
        p[z, :ROWS], p[z, ROWS:] = p_own[z], pa
        q[z, :ROWS], q[z, ROWS:] = q_own[z], qa
        sat = jnp.concatenate([s_own[z], sa], 0)
        mobile = total_mobility(sat)
        s[z], m[z], f0[z] = sat, mobile, sat * sat / water_viscosity / mobile
        return _

    lax.fori_loop(0, NZ, assemble, 0, unroll=NZ // 2)
    last = lanes((SPAN, LANES)) == LANES - 1

    def first(z, carry):
        cz_prev, fz_prev = carry
        up = jnp.minimum(z + 1, NZ - 1)
        kz, pz, mz = k[z], p[z], m[z]
        ax = coefficient(kz, row_next(kz), mz, row_next(mz))
        ay = jnp.where(last, 0.0, coefficient(kz, col_next(kz), mz, col_next(mz)))
        az = jnp.where(z < NZ - 1, vertical_ratio, 0.0) * coefficient(kz, k[up], mz, m[up])
        fx = ax * (pz - row_next(pz))
        fy = ay * (pz - col_next(pz))
        fzz = az * (pz - p[up])
        diag[z] = storage_term + (az + cz_prev) + (ax + row_prev(ax)) + (ay + col_prev(ay))
        r[z] = q[z] - ((fzz - fz_prev) + (fx - row_prev(fx)) + (fy - col_prev(fy)))
        cx[z], cy[z], cz[z] = ax, ay, az
        fpx[z], fpy[z], fpz[z] = fx, fy, fzz
        return az, fzz

    zero = jnp.zeros((SPAN, LANES), F32)
    lax.fori_loop(0, NZ, first, (zero, zero), unroll=NZ // 2)


def middle(cx, cy_in, cz, diag, r_in, fpy_in, packed, far_strip, near_strip,
           sums, z0, v, fpy, fz, fv, s_pack, q_pack, fp_pack, fz_pack, fv_pack,
           cy, inv, r, cy_ends, fp_ends, fz_ends, fv_ends):
    inside_rows, inside_cols = rows_inside(), cols_inside()
    kp, sp, pp, qp = [], [], [], []
    for t in range(TILES):
        ka, sa = halo_rows(t, far_strip, near_strip)
        pa, qa = halo_rows(TILES + t, far_strip, near_strip)
        kp.append(jnp.concatenate([packed[0, t] * inside_cols, ka * inside_rows * inside_cols], 0))
        sp.append(jnp.concatenate([packed[1, t], sa], 0))
        pp.append(jnp.concatenate([packed[2, t], pa], 0))
        qp.append(jnp.concatenate([packed[3, t], qa], 0))
    mp = each(total_mobility, sp)
    tx = each(coefficient, kp, each(row_next, kp), mp, each(row_next, mp))
    ty = each(coefficient, kp, each(col_next, kp), mp, each(col_next, mp))
    tz = each(coefficient, kp, layer_next(kp), mp, layer_next(mp))
    tz = each(lambda c: vertical_ratio * c, tz)
    tz[-1] = jnp.where(lanes((SPAN, LANES)) < LANES - SEG, tz[-1], 0.0)
    terms = (tx, ty, tz)
    dsum = each(lambda x, xp, y, yp, z, zp: storage_term + (z + zp) + (x + xp) + (y + yp), tx, each(row_prev, tx), ty, each(col_prev, ty), tz, layer_prev(tz))
    ip = each(lambda d: 1.0 / d, dsum)
    flows_p = packed_flows(terms, pp)
    rp = each(lambda a, d: a - d, qp, packed_divergence(flows_p))
    zp0 = each(lambda a, b: a * b, rp, ip)
    flows_z = packed_flows(terms, zp0)
    gp = each(lambda a, d: storage_term * a + d, zp0, packed_divergence(flows_z))
    vp = each(lambda a, b, c: (a - b) * c, gp, rp, ip)
    flows_v = packed_flows(terms, vp)
    for t in range(TILES):
        s_pack[t], q_pack[t] = sp[t], qp[t]
        for joined, face in ((cy_ends, ty), (fp_ends, flows_p[1]), (fz_ends, flows_z[1]), (fv_ends, flows_v[1])):
            joined[t] = join_ends(face[t])
        for d in range(3):
            fp_pack[d, t], fz_pack[d, t], fv_pack[d, t] = flows_p[d][t], flows_z[d][t], flows_v[d][t]

    lane = lanes((SPAN, LANES))

    def first(z, _):
        c, f = ends(cy_ends, z), ends(fp_ends, z)
        last = lane == LANES - 1
        cy[z] = jnp.where(last, c, cy_in[z])
        fpy[z] = jnp.where(last, f, fpy_in[z])
        inverse = 1.0 / (diag[z] + jnp.where(last | (lane == 0), c, 0.0))
        res = r_in[z] - jnp.where(last, f, jnp.where(lane == 0, -f, 0.0))
        inv[z], r[z], z0[z] = inverse, res, res * inverse
        return _

    zero = jnp.zeros((SPAN, LANES), F32)
    zero8 = jnp.zeros((ROWS, LANES), F32)
    lax.fori_loop(0, NZ, first, 0, unroll=NZ)

    def second(z, carry):
        fz_prev, rz, zaz, rv, vaz = carry
        up = jnp.minimum(z + 1, NZ - 1)
        a = z0[z]
        fx = cx[z] * (a - row_next(a))
        end = ends(fz_ends, z)
        fy = edge_next(cy[z] * (a - col_next(a)), end)
        fzz = cz[z] * (a - z0[up])
        g = storage_term * a + ((fzz - fz_prev) + (fx - row_prev(fx)) + (fy - edge_prev(fy, end)))
        fz[0, z], fz[1, z], fz[2, z] = fx, fy, fzz
        diff = g - r[z]
        b = diff * inv[z]
        v[z] = b
        a8, g8, d8, b8, r8 = a[:ROWS], g[:ROWS], diff[:ROWS], b[:ROWS], r[z, :ROWS]
        return fzz, rz + r8 * a8, zaz + a8 * g8, rv + a8 * d8, vaz + b8 * g8

    _, rz, zaz, rv, vaz = lax.fori_loop(0, NZ, second, (zero, zero8, zero8, zero8, zero8), unroll=NZ)

    def third(z, carry):
        fz_prev, vav = carry
        up = jnp.minimum(z + 1, NZ - 1)
        a = v[z]
        fx = cx[z] * (a - row_next(a))
        end = ends(fv_ends, z)
        fy = edge_next(cy[z] * (a - col_next(a)), end)
        fzz = cz[z] * (a - v[up])
        fv[0, z], fv[1, z], fv[2, z] = fx, fy, fzz
        w = storage_term * a + ((fzz - fz_prev) + (fx - row_prev(fx)) + (fy - edge_prev(fy, end)))
        return fzz, vav + a[:ROWS] * w[:ROWS]

    _, vav = lax.fori_loop(0, NZ, third, (zero, zero8), unroll=NZ)
    row = zero8
    for i, x in enumerate((rz, zaz, rv, vaz, vav)):
        row = jnp.where(lanes() == i, jnp.sum(x), row)
    for i in range(sums.shape[0] // ROWS):
        sums[i * ROWS:(i + 1) * ROWS] = row


def finish(sums, p_own, z0, v, s, q, f0, fpx, fpy, fpz, fz, fv, s_pack, q_pack, fp_pack, fz_pack, fv_pack,
           pressure_out, s_out, flow, f1, s1, wy0_ends, wy1_ends, pressure, s_new, sems):
    total = jnp.sum(sums[...], axis=0, keepdims=True)
    lane = lanes((1, LANES))
    rz, zaz, rv, vaz, vav = (jnp.sum(jnp.where(lane == i, total, 0.0), axis=1, keepdims=True) for i in range(5))
    ratio = vaz / zaz
    bottom = vav - ratio * vaz
    top = rv - ratio * rz
    good = bottom > 0.0
    b = jnp.where(good, top / jnp.where(good, bottom, 1.0), 0.0)
    a = rz / zaz - b * ratio
    a16, b16 = (jnp.broadcast_to(x, (SPAN, LANES)) for x in (a, b))

    def gained(rate, fraction):
        return jnp.maximum(rate, 0.0) + jnp.minimum(rate, 0.0) * fraction

    def upwind(flux, here, there):
        return flux * jnp.where(flux > 0.0, here, there)

    flows = [[fp_pack[d, t] + a16 * fz_pack[d, t] + b16 * fv_pack[d, t] for t in range(TILES)] for d in range(3)]
    s_now = [s_pack[t] for t in range(TILES)]
    q_now = [q_pack[t] for t in range(TILES)]
    for step, keep in enumerate((wy0_ends, wy1_ends)):
        fr = each(water_fraction, s_now)
        nexts = (each(row_next, fr), each(col_next, fr), layer_next(fr))
        water = [each(upwind, fl, fr, n) for fl, n in zip(flows, nexts)]
        for t in range(TILES):
            keep[t] = join_ends(water[1][t])
        if step == 0:
            s_now = each(lambda x, rate, f, d: x + step_ratio * (gained(rate, f) - d), s_now, q_now, fr, packed_divergence(water))

    def first(z, wz_prev):
        up = jnp.minimum(z + 1, NZ - 1)
        fx, fy, fzz = (fp[z] + a16 * fz[d, z] + b16 * fv[d, z] for d, fp in enumerate((fpx, fpy, fpz)))
        flow[0, z], flow[1, z], flow[2, z] = fx, fy, fzz
        pressure[z] = p_own[z] + a16[:ROWS] * z0[z, :ROWS] + b16[:ROWS] * v[z, :ROWS]
        f = f0[z]
        wx = upwind(fx, f, row_next(f))
        end = ends(wy0_ends, z)
        wy = edge_next(upwind(fy, f, col_next(f)), end)
        wz = upwind(fzz, f, f0[up])
        new = s[z] + step_ratio * (gained(q[z], f) - ((wz - wz_prev) + (wx - row_prev(wx)) + (wy - edge_prev(wy, end))))
        s1[z] = new
        f1[z] = water_fraction(new)
        return wz

    lax.fori_loop(0, NZ, first, jnp.zeros((SPAN, LANES), F32), unroll=NZ)
    send = pltpu.make_async_copy(pressure, pressure_out, sems.at[0])
    send.start()

    def second(z, wz_prev):
        up = jnp.minimum(z + 1, NZ - 1)
        f = f1[z]
        wx = upwind(flow[0, z], f, row_next(f))
        end = ends(wy1_ends, z)
        wy = edge_next(upwind(flow[1, z], f, col_next(f)), end)
        wz = upwind(flow[2, z, :ROWS], f[:ROWS], f1[up, :ROWS])
        east = (wy - edge_prev(wy, end))[:ROWS]
        s_new[z] = s1[z, :ROWS] + step_ratio * (gained(q[z, :ROWS], f[:ROWS]) - ((wz - wz_prev) + (wx - row_prev(wx))[:ROWS] + east))
        return wz

    carry, half, sent = jnp.zeros((ROWS, LANES), F32), NZ // 2, [send]
    for i in range(2):
        carry = lax.fori_loop(i * half, (i + 1) * half, second, carry, unroll=half)
        part = slice(i * half, (i + 1) * half)
        sent.append(pltpu.make_async_copy(s_new.at[part], s_out.at[part], sems.at[1 + i]))
        sent[-1].start()
    for c in sent:
        c.wait()


VMEM = pl.BlockSpec(memory_space=pltpu.VMEM)
ANY = pl.BlockSpec(memory_space=pl.ANY)
SCRATCH = pltpu.CompilerParams(vmem_limit_bytes=8 << 20)


def call(body, outs, args, scratch=()):
    args = [pltpu.with_memory_space_constraint(x, pltpu.VMEM) for x in args]
    return pl.pallas_call(
        body,
        compiler_params=SCRATCH,
        out_shape=tuple(pltpu.VMEM(s, F32) for s in outs),
        in_specs=[VMEM] * len(args),
        out_specs=tuple(VMEM for _ in outs),
        scratch_shapes=[pltpu.VMEM(s, F32) for s in scratch],
    )(*args)


def ring(x, axis, by):
    n = lax.axis_size(axis)
    return lax.ppermute(x, axis, [(i, (i + by) % n) for i in range(n)])


def trade(x, first):
    nx, ny = lax.axis_size("gx"), lax.axis_size("gy")
    other = {}
    for i in range(first, nx - 1, 2):
        other[i], other[i + 1] = i + 1, i
    pairs = [(i * ny + j, other[i] * ny + j if i in other else i * ny + (j ^ 1)) for i in range(nx) for j in range(ny)]
    return lax.ppermute(x, ("gx", "gy"), pairs)


def one_sample(k, s, p, q):
    own = (NZ, ROWS, LANES)
    assert k.shape == own
    cols = (TILES, ROWS, LANES)
    first, last, k, s, p, q = pl.pallas_call(
        pack_columns,
        name="pack_columns",
        compiler_params=SCRATCH,
        out_shape=tuple(pltpu.VMEM(x, F32) for x in (cols, cols, own, own, own, own)),
        in_specs=[ANY] * 4,
        out_specs=(VMEM,) * 6,
        scratch_shapes=[pltpu.SemaphoreType.DMA((4, NZ // PIECE))],
    )(*(pltpu.with_memory_space_constraint(x, pltpu.HBM) for x in (k, s, p, q)))
    from_prev = ring(last, "gy", 1)
    from_next = ring(first, "gy", -1)
    body, strips = (2 * NZ, ROWS, LANES), (2 * TILES, ROWS, LANES)
    to_far, to_near = call(pack_body, (body, body), (k, s, p, q))
    far = trade(to_far, 1)
    near = trade(to_near, 0)
    packed, to_far, to_near = call(pack_strip, ((4,) + cols, strips, strips), (first, last, from_prev, from_next))
    far_strip = trade(to_far, 1)
    near_strip = trade(to_near, 0)
    field, strip = (NZ, SPAN, LANES), (TILES, SPAN, LANES)
    s, q, f0, cx, cy, cz, diag, r, fpx, fpy, fpz = call(interior, (field,) * 11, (k, s, p, q, far, near), (field,) * 3)
    size = lax.axis_size("gx") * lax.axis_size("gy")
    sums, z0, v, fpy, *rest = call(
        middle,
        ((size, LANES),) + (field,) * 3 + ((3,) + field,) * 2 + (strip,) * 2 + ((3,) + strip,) * 3,
        (cx, cy, cz, diag, r, fpy, packed, far_strip, near_strip),
        (field,) * 3 + (strip,) * 4,
    )
    sums = lax.all_to_all(sums, ("gx", "gy"), 0, 0, tiled=True)
    args = [pltpu.with_memory_space_constraint(x, pltpu.VMEM) for x in (sums, p, z0, v, s, q, f0, fpx, fpy, fpz, *rest)]
    return pl.pallas_call(
        finish,
        name="finish",
        compiler_params=SCRATCH,
        out_shape=(jax.ShapeDtypeStruct(own, F32),) * 2,
        in_specs=[VMEM] * len(args),
        out_specs=(ANY, ANY),
        scratch_shapes=[pltpu.VMEM(x, F32) for x in ((3,) + field, field, field, strip, strip, own, own)] + [pltpu.SemaphoreType.DMA((3,))],
    )(*args)


def local(permeability, saturation, pressure_old, source):
    outs = [one_sample(permeability[i], saturation[i], pressure_old[i], source) for i in range(permeability.shape[0])]
    return jnp.stack([o[0] for o in outs]), jnp.stack([o[1] for o in outs])


def solution(mesh):
    field = P(None, None, "gx", "gy")
    return jax.shard_map(local, mesh=mesh, in_specs=(field, field, field, P(None, "gx", "gy")), out_specs=(field, field), check_vma=False)
```

```python
import jax
import jax.numpy as jnp
from jax import lax
from jax.experimental import pallas as pl
from jax.experimental.pallas import tpu as pltpu
from jax.sharding import PartitionSpec as P


storage_term = 0.5
vertical_ratio = 0.1
step_ratio = 0.05
water_viscosity = 1.0
oil_viscosity = 2.0

NZ, ROWS, LANES, HALO = 16, 8, 128, 4
SPAN = 2 * ROWS
SEG = 16
TILES = NZ * SEG // LANES
PER = LANES // SEG
F32 = jnp.float32
PIECE = 8


def lanes(shape=(ROWS, LANES)):
    return lax.broadcasted_iota(jnp.int32, shape, len(shape) - 1)


def sublanes(shape=(ROWS, LANES)):
    return lax.broadcasted_iota(jnp.int32, shape, len(shape) - 2)


def turn(x, by, axis):
    n = x.shape[axis]
    if isinstance(by, int):
        by %= n
        if by == 0:
            return x
    return pltpu.roll(x, by, axis)


def total_mobility(s):
    return s * s / water_viscosity + (1.0 - s) * (1.0 - s) / oil_viscosity


def water_fraction(s):
    return s * s / water_viscosity / total_mobility(s)


def coefficient(ka, kb, ma, mb):
    return ka * kb * (ma + mb) / jnp.maximum(ka + kb, 1e-30)


def row_next(x):
    return turn(x, -1, 0)


def row_prev(x):
    return turn(x, 1, 0)


def col_next(x):
    return turn(x, -1, 1)


def col_prev(x):
    return turn(x, 1, 1)


def pack_columns(k_in, s_in, p_in, q_in, to_prev, to_next, k, s, p, q, sems):
    pieces = range(0, NZ, PIECE)
    copies = [
        [pltpu.make_async_copy(a.at[z:z + PIECE], b.at[z:z + PIECE], sems.at[i, z // PIECE]) for i, (a, b) in enumerate(((k_in, k), (s_in, s), (p_in, p), (q_in, q)))]
        for z in pieces
    ]
    for piece in copies:
        for c in piece:
            c.start()
    quad = lanes() // 4
    quads = LANES // 4
    first = [jnp.zeros((ROWS, LANES), F32) for _ in range(TILES)]
    last = [jnp.zeros((ROWS, LANES), F32) for _ in range(TILES)]
    for z in range(NZ):
        if z % PIECE == 0:
            for c in copies[z // PIECE]:
                c.wait()
        t, zz = divmod(z, PER)
        for i, ref in enumerate((k, s, p, q)):
            at = zz * 4 + i
            x = turn(ref[z], 4 * at + HALO, 1)
            last[t] = jnp.where(quad == at, x, last[t])
            first[t] = jnp.where(quad == (at + 1) % quads, x, first[t])
    for t in range(TILES):
        to_prev[t] = turn(first[t], -HALO, 1)
        to_next[t] = last[t]


def pair(at, a, b, to_far, to_near):
    odd = lax.axis_index("gx") % 2 == 1
    low = sublanes() < HALO
    before = jnp.where(low, a, turn(b, HALO, 0))
    after = jnp.where(low, turn(a, HALO, 0), b)
    to_far[at] = jnp.where(odd, after, before)
    to_near[at] = jnp.where(odd, before, after)


def pack_body(k, s, p, q, to_far, to_near):
    for z in range(NZ):
        pair(z, k[z], s[z], to_far, to_near)
        pair(NZ + z, p[z], q[z], to_far, to_near)


def pack_strip(own_first, own_last, from_prev, from_next, packed, to_far, to_near):
    seg = lanes() % SEG // 4
    for t in range(TILES):
        cols = []
        for i in range(4):
            x = turn(from_prev[t], -4 * i, 1)
            x = jnp.where(seg == 1, turn(own_first[t], 4 - 4 * i, 1), x)
            x = jnp.where(seg == 2, turn(own_last[t], 8 - 4 * i, 1), x)
            x = jnp.where(seg == 3, turn(from_next[t], 12 - 4 * i, 1), x)
            packed[i, t] = x
            cols.append(x)
        pair(t, cols[0], cols[1], to_far, to_near)
        pair(TILES + t, cols[2], cols[3], to_far, to_near)


def layer_next(x):
    edge = lanes((SPAN, LANES)) < LANES - SEG
    moved = [turn(t, -SEG, 1) for t in x]
    return [jnp.where(edge, moved[i], moved[(i + 1) % TILES]) for i in range(TILES)]


def layer_prev(x):
    edge = lanes((SPAN, LANES)) >= SEG
    moved = [turn(t, SEG, 1) for t in x]
    return [jnp.where(edge, moved[i], moved[(i - 1) % TILES]) for i in range(TILES)]


def each(f, *args):
    return [f(*a) for a in zip(*args)]


def packed_divergence(flows):
    fx, fy, fz = flows
    return each(lambda x, xp, y, yp, z, zp: (z - zp) + (x - xp) + (y - yp), fx, each(row_prev, fx), fy, each(col_prev, fy), fz, layer_prev(fz))


def packed_flows(terms, v):
    nexts = (each(row_next, v), each(col_next, v), layer_next(v))
    return [each(lambda c, a, b: c * (a - b), term, v, n) for term, n in zip(terms, nexts)]


def join_ends(face):
    behind = lanes((SPAN, LANES)) % SEG == 11
    return jnp.where(behind, face, turn(face, 9, 1))


def ends(joined, z):
    return pltpu.roll(joined[z // PER], LANES - 1 - (z % PER * SEG + 11), 1)


def edge_next(y, end):
    return jnp.where(lanes((SPAN, LANES)) == LANES - 1, end, y)


def edge_prev(y, end):
    return jnp.where(lanes((SPAN, LANES)) == 0, end, col_prev(y))


def rows_inside():
    gx = lax.axis_index("gx")
    below = jnp.where(gx == lax.axis_size("gx") - 1, 0.0, 1.0)
    return jnp.where(sublanes() < HALO, below, jnp.where(gx == 0, 0.0, 1.0))


def cols_inside():
    gy = lax.axis_index("gy")
    after = jnp.where(gy == lax.axis_size("gy") - 1, 0.0, 1.0)
    seg = lanes() % SEG // 4
    return jnp.where(seg == 0, jnp.where(gy == 0, 0.0, 1.0), jnp.where(seg == 3, after, 1.0))


def halo_rows(at, far, near):
    odd = lax.axis_index("gx") % 2 == 1
    low = sublanes() < HALO
    below, above = jnp.where(odd, far[at], near[at]), jnp.where(odd, near[at], far[at])
    return jnp.where(low, below, turn(above, HALO, 0)), jnp.where(low, turn(below, HALO, 0), above)


def interior(k_own, s_own, p_own, q_own, far, near, s, q, f0, cx, cy, cz, diag, r, fpx, fpy, fpz, k, p, m):
    inside_rows = rows_inside()

    def assemble(z, _):
        ka, sa = halo_rows(z, far, near)
        pa, qa = halo_rows(NZ + z, far, near)
        k[z, :ROWS], k[z, ROWS:] = k_own[z], ka * inside_rows
        p[z, :ROWS], p[z, ROWS:] = p_own[z], pa
        q[z, :ROWS], q[z, ROWS:] = q_own[z], qa
        sat = jnp.concatenate([s_own[z], sa], 0)
        mobile = total_mobility(sat)
        s[z], m[z], f0[z] = sat, mobile, sat * sat / water_viscosity / mobile
        return _

    lax.fori_loop(0, NZ, assemble, 0, unroll=NZ // 2)
    last = lanes((SPAN, LANES)) == LANES - 1

    def first(z, carry):
        cz_prev, fz_prev = carry
        up = jnp.minimum(z + 1, NZ - 1)
        kz, pz, mz = k[z], p[z], m[z]
        ax = coefficient(kz, row_next(kz), mz, row_next(mz))
        ay = jnp.where(last, 0.0, coefficient(kz, col_next(kz), mz, col_next(mz)))
        az = jnp.where(z < NZ - 1, vertical_ratio, 0.0) * coefficient(kz, k[up], mz, m[up])
        fx = ax * (pz - row_next(pz))
        fy = ay * (pz - col_next(pz))
        fzz = az * (pz - p[up])
        diag[z] = storage_term + (az + cz_prev) + (ax + row_prev(ax)) + (ay + col_prev(ay))
        r[z] = q[z] - ((fzz - fz_prev) + (fx - row_prev(fx)) + (fy - col_prev(fy)))
        cx[z], cy[z], cz[z] = ax, ay, az
        fpx[z], fpy[z], fpz[z] = fx, fy, fzz
        return az, fzz

    zero = jnp.zeros((SPAN, LANES), F32)
    lax.fori_loop(0, NZ, first, (zero, zero), unroll=NZ // 2)


def middle(cx, cy_in, cz, diag, r_in, fpy_in, packed, far_strip, near_strip,
           sums, z0, v, fpy, fz, fv, s_pack, q_pack, fp_pack, fz_pack, fv_pack,
           cy, inv, r, cy_ends, fp_ends, fz_ends, fv_ends):
    inside_rows, inside_cols = rows_inside(), cols_inside()
    kp, sp, pp, qp = [], [], [], []
    for t in range(TILES):
        ka, sa = halo_rows(t, far_strip, near_strip)
        pa, qa = halo_rows(TILES + t, far_strip, near_strip)
        kp.append(jnp.concatenate([packed[0, t] * inside_cols, ka * inside_rows * inside_cols], 0))
        sp.append(jnp.concatenate([packed[1, t], sa], 0))
        pp.append(jnp.concatenate([packed[2, t], pa], 0))
        qp.append(jnp.concatenate([packed[3, t], qa], 0))
    mp = each(total_mobility, sp)
    tx = each(coefficient, kp, each(row_next, kp), mp, each(row_next, mp))
    ty = each(coefficient, kp, each(col_next, kp), mp, each(col_next, mp))
    tz = each(coefficient, kp, layer_next(kp), mp, layer_next(mp))
    tz = each(lambda c: vertical_ratio * c, tz)
    tz[-1] = jnp.where(lanes((SPAN, LANES)) < LANES - SEG, tz[-1], 0.0)
    terms = (tx, ty, tz)
    dsum = each(lambda x, xp, y, yp, z, zp: storage_term + (z + zp) + (x + xp) + (y + yp), tx, each(row_prev, tx), ty, each(col_prev, ty), tz, layer_prev(tz))
    ip = each(lambda d: 1.0 / d, dsum)
    flows_p = packed_flows(terms, pp)
    rp = each(lambda a, d: a - d, qp, packed_divergence(flows_p))
    zp0 = each(lambda a, b: a * b, rp, ip)
    flows_z = packed_flows(terms, zp0)
    gp = each(lambda a, d: storage_term * a + d, zp0, packed_divergence(flows_z))
    vp = each(lambda a, b, c: (a - b) * c, gp, rp, ip)
    flows_v = packed_flows(terms, vp)
    for t in range(TILES):
        s_pack[t], q_pack[t] = sp[t], qp[t]
        for joined, face in ((cy_ends, ty), (fp_ends, flows_p[1]), (fz_ends, flows_z[1]), (fv_ends, flows_v[1])):
            joined[t] = join_ends(face[t])
        for d in range(3):
            fp_pack[d, t], fz_pack[d, t], fv_pack[d, t] = flows_p[d][t], flows_z[d][t], flows_v[d][t]

    lane = lanes((SPAN, LANES))

    def first(z, _):
        c, f = ends(cy_ends, z), ends(fp_ends, z)
        last = lane == LANES - 1
        cy[z] = jnp.where(last, c, cy_in[z])
        fpy[z] = jnp.where(last, f, fpy_in[z])
        inverse = 1.0 / (diag[z] + jnp.where(last | (lane == 0), c, 0.0))
        res = r_in[z] - jnp.where(last, f, jnp.where(lane == 0, -f, 0.0))
        inv[z], r[z], z0[z] = inverse, res, res * inverse
        return _

    zero = jnp.zeros((SPAN, LANES), F32)
    zero8 = jnp.zeros((ROWS, LANES), F32)
    lax.fori_loop(0, NZ, first, 0, unroll=NZ)

    def second(z, carry):
        fz_prev, rz, zaz, rv, vaz = carry
        up = jnp.minimum(z + 1, NZ - 1)
        a = z0[z]
        fx = cx[z] * (a - row_next(a))
        end = ends(fz_ends, z)
        fy = edge_next(cy[z] * (a - col_next(a)), end)
        fzz = cz[z] * (a - z0[up])
        g = storage_term * a + ((fzz - fz_prev) + (fx - row_prev(fx)) + (fy - edge_prev(fy, end)))
        fz[0, z], fz[1, z], fz[2, z] = fx, fy, fzz
        diff = g - r[z]
        b = diff * inv[z]
        v[z] = b
        a8, g8, d8, b8, r8 = a[:ROWS], g[:ROWS], diff[:ROWS], b[:ROWS], r[z, :ROWS]
        return fzz, rz + r8 * a8, zaz + a8 * g8, rv + a8 * d8, vaz + b8 * g8

    _, rz, zaz, rv, vaz = lax.fori_loop(0, NZ, second, (zero, zero8, zero8, zero8, zero8), unroll=NZ)

    def third(z, carry):
        fz_prev, vav = carry
        up = jnp.minimum(z + 1, NZ - 1)
        a = v[z]
        fx = cx[z] * (a - row_next(a))
        end = ends(fv_ends, z)
        fy = edge_next(cy[z] * (a - col_next(a)), end)
        fzz = cz[z] * (a - v[up])
        fv[0, z], fv[1, z], fv[2, z] = fx, fy, fzz
        w = storage_term * a + ((fzz - fz_prev) + (fx - row_prev(fx)) + (fy - edge_prev(fy, end)))
        return fzz, vav + a[:ROWS] * w[:ROWS]

    _, vav = lax.fori_loop(0, NZ, third, (zero, zero8), unroll=NZ)
    row = zero8
    for i, x in enumerate((rz, zaz, rv, vaz, vav)):
        row = jnp.where(lanes() == i, jnp.sum(x), row)
    for i in range(sums.shape[0] // ROWS):
        sums[i * ROWS:(i + 1) * ROWS] = row


def finish(sums, p_own, z0, v, s, q, f0, fpx, fpy, fpz, fz, fv, s_pack, q_pack, fp_pack, fz_pack, fv_pack,
           pressure_out, s_out, flow, f1, s1, wy0_ends, wy1_ends, pressure, s_new, sems):
    parts = [sums[i:i + ROWS] for i in range(0, sums.shape[0], ROWS)]
    while len(parts) > 1:
        parts = [sum(parts[i + 1:i + 2], parts[i]) for i in range(0, len(parts), 2)]
    total = jnp.sum(parts[0], axis=0, keepdims=True)
    lane = lanes((1, LANES))
    rz, zaz, rv, vaz, vav = (jnp.sum(jnp.where(lane == i, total, 0.0), axis=1, keepdims=True) for i in range(5))
    ratio = vaz / zaz
    bottom = vav - ratio * vaz
    top = rv - ratio * rz
    good = bottom > 0.0
    b = jnp.where(good, top / jnp.where(good, bottom, 1.0), 0.0)
    a = rz / zaz - b * ratio
    a16, b16 = (jnp.broadcast_to(x, (SPAN, LANES)) for x in (a, b))

    def gained(rate, fraction):
        return jnp.maximum(rate, 0.0) + jnp.minimum(rate, 0.0) * fraction

    def upwind(flux, here, there):
        return flux * jnp.where(flux > 0.0, here, there)

    flows = [[fp_pack[d, t] + a16 * fz_pack[d, t] + b16 * fv_pack[d, t] for t in range(TILES)] for d in range(3)]
    s_now = [s_pack[t] for t in range(TILES)]
    q_now = [q_pack[t] for t in range(TILES)]
    for step, keep in enumerate((wy0_ends, wy1_ends)):
        fr = each(water_fraction, s_now)
        nexts = (each(row_next, fr), each(col_next, fr), layer_next(fr))
        water = [each(upwind, fl, fr, n) for fl, n in zip(flows, nexts)]
        for t in range(TILES):
            keep[t] = join_ends(water[1][t])
        if step == 0:
            s_now = each(lambda x, rate, f, d: x + step_ratio * (gained(rate, f) - d), s_now, q_now, fr, packed_divergence(water))

    def first(z, wz_prev):
        up = jnp.minimum(z + 1, NZ - 1)
        fx, fy, fzz = (fp[z] + a16 * fz[d, z] + b16 * fv[d, z] for d, fp in enumerate((fpx, fpy, fpz)))
        flow[0, z], flow[1, z], flow[2, z] = fx, fy, fzz
        pressure[z] = p_own[z] + a16[:ROWS] * z0[z, :ROWS] + b16[:ROWS] * v[z, :ROWS]
        f = f0[z]
        wx = upwind(fx, f, row_next(f))
        end = ends(wy0_ends, z)
        wy = edge_next(upwind(fy, f, col_next(f)), end)
        wz = upwind(fzz, f, f0[up])
        new = s[z] + step_ratio * (gained(q[z], f) - ((wz - wz_prev) + (wx - row_prev(wx)) + (wy - edge_prev(wy, end))))
        s1[z] = new
        f1[z] = water_fraction(new)
        return wz

    lax.fori_loop(0, NZ, first, jnp.zeros((SPAN, LANES), F32), unroll=NZ)
    send = pltpu.make_async_copy(pressure, pressure_out, sems.at[0])
    send.start()

    def second(z, wz_prev):
        up = jnp.minimum(z + 1, NZ - 1)
        f = f1[z]
        wx = upwind(flow[0, z], f, row_next(f))
        end = ends(wy1_ends, z)
        wy = edge_next(upwind(flow[1, z], f, col_next(f)), end)
        wz = upwind(flow[2, z, :ROWS], f[:ROWS], f1[up, :ROWS])
        east = (wy - edge_prev(wy, end))[:ROWS]
        s_new[z] = s1[z, :ROWS] + step_ratio * (gained(q[z, :ROWS], f[:ROWS]) - ((wz - wz_prev) + (wx - row_prev(wx))[:ROWS] + east))
        return wz

    carry, half, sent = jnp.zeros((ROWS, LANES), F32), NZ // 2, [send]
    for i in range(2):
        carry = lax.fori_loop(i * half, (i + 1) * half, second, carry, unroll=half)
        part = slice(i * half, (i + 1) * half)
        sent.append(pltpu.make_async_copy(s_new.at[part], s_out.at[part], sems.at[1 + i]))
        sent[-1].start()
    for c in sent:
        c.wait()


VMEM = pl.BlockSpec(memory_space=pltpu.VMEM)
ANY = pl.BlockSpec(memory_space=pl.ANY)
SCRATCH = pltpu.CompilerParams(vmem_limit_bytes=8 << 20)


def call(body, outs, args, scratch=()):
    args = [pltpu.with_memory_space_constraint(x, pltpu.VMEM) for x in args]
    return pl.pallas_call(
        body,
        compiler_params=SCRATCH,
        out_shape=tuple(pltpu.VMEM(s, F32) for s in outs),
        in_specs=[VMEM] * len(args),
        out_specs=tuple(VMEM for _ in outs),
        scratch_shapes=[pltpu.VMEM(s, F32) for s in scratch],
    )(*args)


def ring(x, axis, by):
    n = lax.axis_size(axis)
    return lax.ppermute(x, axis, [(i, (i + by) % n) for i in range(n)])


def trade(x, first):
    nx, ny = lax.axis_size("gx"), lax.axis_size("gy")
    other = {}
    for i in range(first, nx - 1, 2):
        other[i], other[i + 1] = i + 1, i
    pairs = [(i * ny + j, other[i] * ny + j if i in other else i * ny + (j ^ 1)) for i in range(nx) for j in range(ny)]
    return lax.ppermute(x, ("gx", "gy"), pairs)


def one_sample(k, s, p, q):
    own = (NZ, ROWS, LANES)
    assert k.shape == own
    cols = (TILES, ROWS, LANES)
    first, last, k, s, p, q = pl.pallas_call(
        pack_columns,
        name="pack_columns",
        compiler_params=SCRATCH,
        out_shape=tuple(pltpu.VMEM(x, F32) for x in (cols, cols, own, own, own, own)),
        in_specs=[ANY] * 4,
        out_specs=(VMEM,) * 6,
        scratch_shapes=[pltpu.SemaphoreType.DMA((4, NZ // PIECE))],
    )(*(pltpu.with_memory_space_constraint(x, pltpu.HBM) for x in (k, s, p, q)))
    from_prev = ring(last, "gy", 1)
    from_next = ring(first, "gy", -1)
    body, strips = (2 * NZ, ROWS, LANES), (2 * TILES, ROWS, LANES)
    to_far, to_near = call(pack_body, (body, body), (k, s, p, q))
    far = trade(to_far, 1)
    near = trade(to_near, 0)
    packed, to_far, to_near = call(pack_strip, ((4,) + cols, strips, strips), (first, last, from_prev, from_next))
    far_strip = trade(to_far, 1)
    near_strip = trade(to_near, 0)
    field, strip = (NZ, SPAN, LANES), (TILES, SPAN, LANES)
    s, q, f0, cx, cy, cz, diag, r, fpx, fpy, fpz = call(interior, (field,) * 11, (k, s, p, q, far, near), (field,) * 3)
    size = lax.axis_size("gx") * lax.axis_size("gy")
    sums, z0, v, fpy, *rest = call(
        middle,
        ((size, LANES),) + (field,) * 3 + ((3,) + field,) * 2 + (strip,) * 2 + ((3,) + strip,) * 3,
        (cx, cy, cz, diag, r, fpy, packed, far_strip, near_strip),
        (field,) * 3 + (strip,) * 4,
    )
    sums = lax.all_to_all(sums, ("gx", "gy"), 0, 0, tiled=True)
    args = [pltpu.with_memory_space_constraint(x, pltpu.VMEM) for x in (sums, p, z0, v, s, q, f0, fpx, fpy, fpz, *rest)]
    return pl.pallas_call(
        finish,
        name="finish",
        compiler_params=SCRATCH,
        out_shape=(jax.ShapeDtypeStruct(own, F32),) * 2,
        in_specs=[VMEM] * len(args),
        out_specs=(ANY, ANY),
        scratch_shapes=[pltpu.VMEM(x, F32) for x in ((3,) + field, field, field, strip, strip, own, own)] + [pltpu.SemaphoreType.DMA((3,))],
    )(*args)


def local(permeability, saturation, pressure_old, source):
    outs = [one_sample(permeability[i], saturation[i], pressure_old[i], source) for i in range(permeability.shape[0])]
    return jnp.stack([o[0] for o in outs]), jnp.stack([o[1] for o in outs])


def solution(mesh):
    field = P(None, None, "gx", "gy")
    return jax.shard_map(local, mesh=mesh, in_specs=(field, field, field, P(None, "gx", "gy")), out_specs=(field, field), check_vma=False)
```
